1024 devices in a mesh: gx: 16 (over y, z_lo), gy: 8 (over x), gz: 8 (over z_hi, core).
Axes of the slice: x: 8, y: 8, z: 8 (z_hi: 4, z_lo: 2; z = z_hi * 2 + z_lo), core: 2. Of those that a mesh axis runs over, the one named last changes fastest.
Arguments:
- positions: float32 [3, 16, 8, 8, 512], P(None, 'gx', 'gy', 'gz'), may hold values from 0 to 1
- velocities: float32 [3, 16, 8, 8, 512], P(None, 'gx', 'gy', 'gz'), may hold values from -1.8 to 1.8
- forces: float32 [3, 16, 8, 8, 512], P(None, 'gx', 'gy', 'gz'), may hold values from -6 to 6
- charges: float32 [16, 8, 8, 512], P('gx', 'gy', 'gz'), may hold values from -4 to 4
- atom_types: int32 [16, 8, 8, 512], P('gx', 'gy', 'gz'), may hold values from 0 to 31
- tile_counts: int32 [16, 8, 8], P('gx', 'gy', 'gz'), may hold values from 1 to 4, as said below
- pair_epsilon: float32 [32], replicated, may hold values from 0.01 to 0.1
- pair_sigma: float32 [32], replicated, may hold values from 0.1 to 0.15
Outputs:
- final_positions: float32 [3, 16, 8, 8, 512], P(None, 'gx', 'gy', 'gz')
- final_velocities: float32 [3, 16, 8, 8, 512], P(None, 'gx', 'gy', 'gz')
- final_forces: float32 [3, 16, 8, 8, 512], P(None, 'gx', 'gy', 'gz')
The draws below stay inside these ranges and needn't reach their ends.
Inputs may be any that keep to these rules, and one draw needn't show every extreme that they name: The live atoms of a box are its first 128 times tile_counts slots; some box has 4 live tiles in every draw.
All inputs are finite; a program needn't handle non-finite values.
Results may differ from the reference program's by a relative error of at most 0.0003.
Values sent between devices are 32-bit elements; how exact they have to be, the bound alone decides.
A program may use at most 32 MiB of HBM per device.

```python
import math
import jax
import jax.numpy as jnp
from jax import lax

TILE = 128
TILES_MAX = 4
NTYPES = 32
STEPS = 2
SLOTS = 512
NGX = 16
NGY = 8
NGZ = 8


def draw_tile_counts(key, part):
    first, second = jax.random.split(key)
    heavy = jax.random.randint(first, (NGX, NGY, NGZ), 0, 4) == 0
    light = jax.random.randint(second, (NGX, NGY, NGZ), 1, max(TILES_MAX, 2))
    counts = jnp.where(heavy, TILES_MAX, light).astype(jnp.int32)
    return counts.at[0, 0, 0].set(TILES_MAX)


def touch_ends(entries, key, low, high):
    spot = [jax.random.randint(jax.random.fold_in(key, axis), (), 0, length) for axis, length in enumerate(entries.shape)]
    main_axis = entries.shape.index(max(entries.shape))
    beside = spot[:main_axis] + [(spot[main_axis] + 1) % entries.shape[main_axis]] + spot[main_axis + 1:]
    return entries.at[tuple(spot)].set(low).at[tuple(beside)].set(high)


def levels(rng, dims, cuts, least, largest):
    factor_of, own = 1.0, jax.random.fold_in(rng, 6)
    for dim, parts in cuts:
        draws = jnp.exp(jax.random.uniform(jax.random.fold_in(own, dim), (parts,), jnp.float32, least / len(cuts), largest / len(cuts)))
        factor_of = factor_of * jnp.repeat(draws, dims[dim] // parts).reshape([-1 if axis == dim else 1 for axis in range(len(dims))])
    return factor_of


def noise(key, dims, spread, most, cuts=(), held_as=jnp.bfloat16):
    values = jax.random.normal(key, dims, jnp.float32) * spread
    if len(cuts) > 0:
        values = levels(key, dims, cuts, -0.22, 0.18) * values
    return jnp.clip(values, min=-most, max=most).astype(held_as)


def setup_inputs(seed: int = 0) -> dict:
    keys = jax.random.split(jax.random.key(seed), 9)
    positions = jnp.clip(1.0 * jax.random.uniform(keys[0], (3, NGX, NGY, NGZ, SLOTS), jnp.float32) ** levels(keys[0], (3, NGX, NGY, NGZ, SLOTS), ((1, 16), (2, 8), (3, 8)), -0.2, 0.2), 0.0, 1.0)
    velocities = noise(keys[1], (3, NGX, NGY, NGZ, SLOTS), 0.3, 1.8, ((1, 16), (2, 8), (3, 8)), jnp.float32)
    forces = noise(keys[2], (3, NGX, NGY, NGZ, SLOTS), 1.0, 6.0, ((1, 16), (2, 8), (3, 8)), jnp.float32)
    charges = noise(keys[3], (NGX, NGY, NGZ, SLOTS), 1.0, 4.0, ((0, 16), (1, 8), (2, 8)), jnp.float32)
    atom_types = touch_ends(jax.random.randint(keys[4], (NGX, NGY, NGZ, SLOTS), 0, NTYPES), jax.random.fold_in(keys[4], 1), 0, NTYPES - 1).astype(jnp.int32)
    tile_counts = draw_tile_counts(jax.random.fold_in(keys[8], 71), 0)
    pair_epsilon = jnp.clip(jnp.exp(jax.random.uniform(keys[6], (NTYPES,), jnp.float32, math.log(0.01), math.log(0.1))), 0.01, 0.1)
    pair_sigma = jnp.clip(jax.random.uniform(keys[7], (NTYPES,), jnp.float32, 0.1, 0.15), 0.1, 0.15)
    return dict(positions=positions, velocities=velocities, forces=forces, charges=charges, atom_types=atom_types, tile_counts=tile_counts, pair_epsilon=pair_epsilon, pair_sigma=pair_sigma)


COULOMB = 0.02
KAPPA = 2.0
SOFTEN = 0.0225
CUTOFF = 0.81
TIME_STEP = 0.05
HALF_STEP = 0.025
HALF_PLATE = ((1, 0), (1, 1), (0, 1), (-1, 1))

def pair_energy(left_pos, right_pos, left_par, right_par, weight):
    diff = left_pos[:, :, None] - right_pos[:, None, :]
    distance = lax.optimization_barrier(jnp.sum(diff * diff, axis=0))
    soft_sq = distance + SOFTEN
    soft = jnp.sqrt(soft_sq)
    coulomb = COULOMB * left_par[0][:, None] * right_par[0][None, :] * jnp.exp(-KAPPA * soft) / soft
    sigma = 0.5 * (left_par[2][:, None] + right_par[2][None, :])
    ratio = sigma * sigma / soft_sq
    cubed = ratio * ratio * ratio
    lennard = 4.0 * left_par[1][:, None] * right_par[1][None, :] * (cubed * cubed - cubed)
    switch = jnp.square(jnp.maximum(1.0 - distance / CUTOFF, 0.0))
    return jnp.sum(weight * (coulomb + lennard) * switch)

def tile_pair(left, right, weight):

    def energy(left_pos, right_pos):
        return pair_energy(left_pos, right_pos, left[3:], right[3:], weight)
    value, pull = jax.vjp(energy, left[:3], right[:3])
    grad_left, grad_right = pull(jnp.ones_like(value))
    return (-grad_left, -grad_right)

def padded_forces(left, right, halve):
    tiles = left.shape[1] // TILE
    width = right.shape[1]
    pieces = left.reshape(6, tiles, TILE).transpose(1, 0, 2)
    starts = jnp.arange(tiles, dtype=jnp.int32) * TILE

    def visit(carry, item):
        piece, start = item
        if halve:
            rows = start + lax.broadcasted_iota(jnp.int32, (TILE, width), 0)
            cols = lax.broadcasted_iota(jnp.int32, (TILE, width), 1)
            weight = jnp.where(rows != cols, 0.5, 0.0).astype(left.dtype)
        else:
            weight = jnp.ones((), left.dtype)
        force_left, force_right = tile_pair(piece, right, weight)
        return (carry + force_right, force_left)
    force_right, stacked = lax.scan(visit, jnp.zeros((3, width), left.dtype), (pieces, starts))
    return (stacked.transpose(1, 0, 2).reshape(3, tiles * TILE), force_right)

def box_forces(tower, plate, own, above):
    force_tower, force_plate = padded_forces(tower, plate, False)
    force_above, force_own = padded_forces(above, own, False)
    self_left, self_right = padded_forces(own, own, True)
    return (force_tower, force_plate, force_above, force_own + self_left + self_right)

def neighbour(record, along_x, along_y, along_z):
    moved = jnp.roll(record, (-along_x, -along_y, -along_z), axis=(1, 2, 3))
    shift = jnp.array([along_x, along_y, along_z], dtype=record.dtype)
    return jnp.concatenate([moved[:3] + shift[:, None, None, None, None], moved[3:]], 0)

def total_forces(record):
    boxes = NGX * NGY * NGZ
    group = math.gcd(boxes, 16)
    slots = record.shape[-1]
    below = neighbour(record, 0, 0, -1)
    above = neighbour(record, 0, 0, 1)
    tower = jnp.concatenate([below, record, above], 4)
    plate = jnp.concatenate([neighbour(record, along_x, along_y, 0) for along_x, along_y in HALF_PLATE], 4)

    def flatten(array):
        width = array.shape[-1]
        return array.reshape(6, boxes, width).transpose(1, 0, 2).reshape(boxes // group, group, 6, width)

    def unflatten(array):
        width = array.shape[-1]
        return array.reshape(boxes, 3, width).transpose(1, 0, 2).reshape(3, NGX, NGY, NGZ, width)

    def batch(items):
        return jax.vmap(box_forces)(*items)
    force_tower, force_plate, force_above, force_own = lax.map(batch, (flatten(tower), flatten(plate), flatten(record), flatten(above)))
    force_tower = unflatten(force_tower)
    force_plate = unflatten(force_plate)
    total = unflatten(force_own) + force_tower[..., slots:2 * slots]
    total = total + jnp.roll(force_tower[..., :slots], -1, axis=3)
    total = total + jnp.roll(force_tower[..., 2 * slots:] + unflatten(force_above), 1, axis=3)
    for number, (along_x, along_y) in enumerate(HALF_PLATE):
        part = force_plate[..., number * slots:(number + 1) * slots]
        total = total + jnp.roll(part, (along_x, along_y), axis=(1, 2))
    return total

def reference(positions, velocities, forces, charges, atom_types, tile_counts, pair_epsilon, pair_sigma):
    index = jnp.arange(SLOTS, dtype=jnp.int32)
    live = (index < tile_counts[..., None] * TILE).astype(positions.dtype)
    kinds = jnp.arange(NTYPES, dtype=jnp.int32)[:, None, None, None, None]
    member = (atom_types[None] == kinds).astype(positions.dtype)
    root = lax.optimization_barrier(jnp.sum(member * jnp.sqrt(pair_epsilon)[:, None, None, None, None], 0)) * live
    sigma = lax.optimization_barrier(jnp.sum(member * pair_sigma[:, None, None, None, None], 0))
    params = jnp.stack([charges * live, root, sigma], 0)
    places, velocity, pushing = (positions, velocities, forces)
    for step in range(STEPS):
        velocity = velocity + HALF_STEP * pushing
        places = places + TIME_STEP * velocity
        pushing = total_forces(jnp.concatenate([places, params], 0))
        velocity = velocity + HALF_STEP * pushing
    return (places, velocity, pushing)
```

```python
import functools

import jax
import jax.numpy as jnp
from jax import lax
from jax.experimental import pallas as pl
from jax.experimental.pallas import tpu as pltpu
from jax.sharding import PartitionSpec as P

TILE = 128
STEPS = 2
TIME_STEP = 0.05
HALF_STEP = 0.025
PLATE = ((1, 0), (1, 1), (0, 1), (-1, 1))
NP = len(PLATE)
OFFSETS = tuple((x, y, 0) for x, y in PLATE) + ((0, 0, -1), (0, 0, 1))
NBR = NP + 2
AXES = ("gx", "gy", "gz")
MESH = pl.DeviceIdType.MESH
F32 = jnp.float32
BF16 = jnp.bfloat16
FAR = 1e6
RB = NP + 2
UN = 4
LOG2E = 1.4426950408889634
FORCE = 8.0 / (3.24 * 3.24)

def pair_kernel(joined, pos_ref, par_ref, own_ref, ownpar_ref, fout_ref, fown_ref,
                left, right, acc_left, list_v, list_s, sem):
    position = (lambda k: pos_ref[k, 0]) if joined else (lambda k: pos_ref[k])
    lane16 = lax.broadcasted_iota(jnp.int32, (1, 16), 1)
    row16 = lax.broadcasted_iota(jnp.int32, (16, 1), 0)
    for k in range(RB):
        if k < NP:
            p = position(k) + jnp.where(row16 < 4, float(PLATE[k][0]), jnp.where(row16 < 8, float(PLATE[k][1]), 0.0))
            a = par_ref[k, 1]
        else:
            p = own_ref[0] if joined else own_ref[...]
            a = ownpar_ref[1]
        p = p * 2.0
        for f in range(3):
            right[f, 4 * k:4 * k + 4, :] = p[4 * f:4 * f + 4]
            right[3 + f, 4 * k:4 * k + 4, :] = a[4 * f:4 * f + 4]
    mins, maxs = [], []
    qscale = jnp.where(lane16 < 4, 0.04 / 6.0 * FORCE, jnp.where(lane16 < 8, 4.0 * FORCE, 1.0))
    for box in range(3):
        if box == 1:
            p, a = (own_ref[0] if joined else own_ref[...]), ownpar_ref[1]
        else:
            slot = NP if box == 0 else NP + 1
            p = position(slot) + jnp.where((row16 >= 8) & (row16 < 12), -1.0 if box == 0 else 1.0, 0.0)
            a = par_ref[slot, 1]
        tp = jnp.transpose(jnp.concatenate([p * 2.0, a], 0), (1, 0))
        lo = tp[:, :16].reshape(4, 32, 16)
        mins.append(jnp.min(lo, axis=1))
        maxs.append(jnp.max(lo, axis=1))
        ta = tp[:, 16:] * qscale
        for t in range(4):
            base = (t * 16 + box * 4) * 4
            for f in range(6):
                col = tp[:, 4 * f + t:4 * f + t + 1] if f < 3 else ta[:, 4 * (f - 3) + t:4 * (f - 3) + t + 1]
                left[f, base:base + 16] = jnp.broadcast_to(col, (128, 128)).reshape(16, 8, 128)
    for f in range(6):
        left[f, 48:64] = jnp.full((16, 8, 128), FAR if f < 3 else 0.0, F32)
    acc_left[...] = jnp.zeros_like(acc_left)
    lmin = jnp.concatenate(mins + [jnp.full((4, 16), FAR, F32)], 0)
    lmax = jnp.concatenate(maxs + [jnp.full((4, 16), FAR, F32)], 0)
    rows = 4 * RB
    d2 = jnp.zeros((64, 128), F32)
    live = None
    for f in range(3):
        a0 = jnp.concatenate([lmin[:, 4 * f + t:4 * f + t + 1] for t in range(4)], 0)
        a1 = jnp.concatenate([lmax[:, 4 * f + t:4 * f + t + 1] for t in range(4)], 0)
        v = jnp.concatenate([right[f, :rows, :], jnp.full((128 - rows, 128), FAR, F32)], 0)
        b0 = jnp.transpose(jnp.broadcast_to(jnp.min(v, axis=1, keepdims=True), (128, 128)), (1, 0))[:1]
        b1 = jnp.transpose(jnp.broadcast_to(jnp.max(v, axis=1, keepdims=True), (128, 128)), (1, 0))[:1]
        gap = jnp.maximum(jnp.maximum(a0 - b1, b0 - a1), 0.0)
        d2 = d2 + gap * gap
        if f == 0:
            live = a0 < 0.1 * FAR
    row = lax.broadcasted_iota(jnp.int32, (64, 128), 0)
    col = lax.broadcasted_iota(jnp.int32, (64, 128), 1)
    lt, lbox = row // 16, (row // 4) % 4
    rbox, rt = col // 4, col % 4
    plate = (rbox < NP) & (lbox < 3)
    inner = (rbox == NP) & ((lbox == 2) | ((lbox == 1) & (lt < rt)))
    diag = (rbox == NP + 1) & (lbox == 1) & (lt == rt)
    m = (d2 < 3.2401) & live & (plate | inner | diag)
    mf = m.astype(BF16)
    r64 = lax.broadcasted_iota(jnp.int32, (64, 64), 0)
    c64 = lax.broadcasted_iota(jnp.int32, (64, 64), 1)
    before = jnp.dot((c64 < r64).astype(BF16), mf, preferred_element_type=F32)
    place = jnp.where(m, before.astype(jnp.int32), -1)
    count = jnp.sum(m.astype(jnp.int32), axis=0, keepdims=True)
    value = row - 12
    for k in range(48):
        list_v[k:k + 1, :] = jnp.sum(jnp.where(place == k, value, 0), axis=0, keepdims=True) + 12
    list_v[48:49, :] = count
    copy = pltpu.make_async_copy(list_v, list_s, sem)
    copy.start()
    copy.wait()

    def one_tile(r, _):
        trips = (list_s[48, r] + (UN - 1)) // UN
        rx, ry, rz, rq, re, rs_ = [jnp.broadcast_to(right[f, pl.ds(r, 1), :], (8, 128))[None] for f in range(6)]

        def body(it, acc):
            ax, ay, az = acc
            for j in range(UN):
                b = list_s[it * UN + j, r] * 4
                dx = left[0, pl.ds(b, 4)] - rx
                dy = left[1, pl.ds(b, 4)] - ry
                dz = left[2, pl.ds(b, 4)] - rz
                s2 = (dx * dx + 0.09) + dy * dy + dz * dz
                rs = lax.rsqrt(s2)
                inv = rs * rs
                ex = jnp.exp2(s2 * (-LOG2E) * rs)
                w = jnp.maximum(3.33 - s2, 0.0)
                bb = (w * inv) * 1.5
                a2 = bb + 1.0
                a1 = a2 + bb
                sg = left[5, pl.ds(b, 4)] + rs_
                tt = sg * sg * inv
                t3 = tt * tt * tt
                ll = (left[4, pl.ds(b, 4)] * re) * t3
                lj = ll * (t3 * a1 - a2)
                cc = (left[3, pl.ds(b, 4)] * rq) * ex * (rs * (a2 + 5.0) + bb)
                g = (lj + cc) * w
                fx, fy, fz = g * dx, g * dy, g * dz
                acc_left[0, pl.ds(b, 4)] += fx
                acc_left[1, pl.ds(b, 4)] += fy
                acc_left[2, pl.ds(b, 4)] += fz
                ax = ax - jnp.sum(fx, axis=0)
                ay = ay - jnp.sum(fy, axis=0)
                az = az - jnp.sum(fz, axis=0)
            return ax, ay, az

        zero = jnp.zeros((8, 128), F32)
        acc = lax.fori_loop(0, trips, body, (zero, zero, zero))
        for f in range(3):
            right[f, pl.ds(r, 1), :] = jnp.sum(acc[f], axis=0, keepdims=True)
        return 0

    lax.fori_loop(0, rows, one_tile, 0)
    zero4 = jnp.zeros((4, 128), F32)
    for k in range(NP):
        fout_ref[k] = jnp.concatenate([right[f, 4 * k:4 * k + 4, :] for f in range(3)] + [zero4], 0)
    ones = jnp.ones((8, 128), BF16)
    for box in range(3):
        out = []
        for f in range(3):
            for t in range(4):
                base = (t * 16 + box * 4) * 4
                a = acc_left[f, base:base + 16].reshape(128, 128)
                hi = a.astype(BF16)
                lo = (a - hi.astype(F32)).astype(BF16)
                dn = (((1,), (1,)), ((), ()))
                v = lax.dot_general(ones, hi, dn, preferred_element_type=F32) + lax.dot_general(ones, lo, dn, preferred_element_type=F32)
                out.append(v[:1])
        out = jnp.concatenate(out + [zero4], 0)
        if box == 1:
            fown_ref[...] = out + jnp.concatenate([right[f, 4 * NP:4 * NP + 4, :] for f in range(3)] + [zero4], 0)
        else:
            fout_ref[NP if box == 0 else NP + 1] = out

def pair_forces(pos, par, own, ownpar, joined):
    v = pl.BlockSpec(memory_space=pltpu.VMEM)
    return pl.pallas_call(
        functools.partial(pair_kernel, joined),
        out_shape=(jax.ShapeDtypeStruct((NBR, 16, 128), F32), jax.ShapeDtypeStruct((16, 128), F32)),
        in_specs=[v] * 4, out_specs=(v, v),
        scratch_shapes=[
            pltpu.VMEM((6, 256, 8, 128), F32),
            pltpu.VMEM((6, -(-4 * RB // 8) * 8, 128), F32),
            pltpu.VMEM((3, 256, 8, 128), F32),
            pltpu.VMEM((56, 128), jnp.int32),
            pltpu.SMEM((56, 128), jnp.int32),
            pltpu.SemaphoreType.DMA,
        ],
        compiler_params=pltpu.CompilerParams(vmem_limit_bytes=32 << 20),
    )(pos, par, own, ownpar)


def hilbert(cells, bits):
    x = list(cells)
    q = 1 << (bits - 1)
    while q > 1:
        p = q - 1
        for i in range(3):
            hit = (x[i] & q) != 0
            if i == 0:
                x[0] = jnp.where(hit, x[0] ^ p, x[0])
            else:
                swap = (x[0] ^ x[i]) & p
                x[0], x[i] = jnp.where(hit, x[0] ^ p, x[0] ^ swap), jnp.where(hit, x[i], x[i] ^ swap)
        q >>= 1
    x[1] = x[1] ^ x[0]
    x[2] = x[2] ^ x[1]
    flip = jnp.zeros_like(x[0])
    q = 1 << (bits - 1)
    while q > 1:
        flip = jnp.where((x[2] & q) != 0, flip ^ (q - 1), flip)
        q >>= 1
    x = [v ^ flip for v in x]
    key = jnp.zeros_like(x[0])
    for bit in range(bits - 1, -1, -1):
        for a in range(3):
            key = key * 2 + ((x[a] >> bit) & 1)
    return key


def split3(a):
    hi = a.astype(BF16)
    rest = a - hi.astype(F32)
    mid = rest.astype(BF16)
    lo = (rest - mid.astype(F32)).astype(BF16)
    return jnp.concatenate([hi, mid, lo], 0)


def chosen(rank, t):
    place = lax.broadcasted_iota(jnp.int32, (TILE, TILE), 0) + TILE * t
    tiles = [(rank[j : j + 1, :] == place).astype(F32).astype(BF16) for j in range(4)]
    return jnp.concatenate(tiles, 1)


def sort_kernel(
    count_ref, eps_ref, sig_ref, pos_ref, vel_ref, frc_ref, chg_ref, typ_ref,
    x_ref, v_ref, rec_ref, rank_ref, stage, staged,
):
    v = vel_ref[...] + HALF_STEP * frc_ref[...]
    x = pos_ref[...] + TIME_STEP * v
    count = count_ref[0, 0]
    row = lax.broadcasted_iota(jnp.int32, (4, TILE), 0)
    live = row < count
    kinds = typ_ref[...]
    eps = jnp.zeros((4, TILE), F32)
    sig = jnp.zeros((4, TILE), F32)
    for k in range(eps_ref.shape[0]):
        eps = jnp.where(kinds == k, eps_ref[k], eps)
        sig = jnp.where(kinds == k, sig_ref[k], sig)
    alive = live.astype(F32)
    stage[...] = jnp.zeros_like(stage)
    stage[0:12, :] = x
    stage[12:24, :] = v
    stage[24:28, :] = chg_ref[...] * alive
    stage[28:32, :] = jnp.sqrt(eps) * alive
    stage[32:36, :] = sig
    cells = [
        jnp.clip((jnp.clip(x[4 * a : 4 * a + 4], -1.0, 2.0) * 4.0).astype(jnp.int32), 0, 3)
        for a in range(3)
    ]
    index = row * TILE + lax.broadcasted_iota(jnp.int32, (4, TILE), 1)
    key = jnp.where(live, hilbert(cells, 2), 64) * 512 + index
    key = jnp.concatenate([key.astype(F32), jnp.zeros((4, TILE), F32)], 0)
    down = jnp.transpose(key, (1, 0))
    ranks = []
    for j in range(4):
        less = jnp.zeros((TILE, TILE), F32)
        for i in range(4):
            less = less + (down[:, i : i + 1] < key[j : j + 1, :]).astype(F32)
        ranks.append(jnp.sum(less, axis=0, keepdims=True))
    rank = jnp.concatenate(ranks, 0).astype(jnp.int32)
    rank_ref[...] = rank
    fields = jnp.concatenate([stage[pl.ds(t, 16, stride=4), :] for t in range(4)], 1)
    parts = split3(fields)
    for t in range(4):
        out = lax.dot_general(
            parts, chosen(rank, t), (((1,), (1,)), ((), ())), preferred_element_type=F32
        )
        staged[pl.ds(t, 16, stride=4), :] = (out[32:48] + out[16:32]) + out[0:16]
    row16 = lax.broadcasted_iota(jnp.int32, (16, TILE), 0)
    place = staged[0:16, :]
    x_ref[...] = place
    v_ref[...] = staged[12:28, :]
    rec_ref[0] = jnp.where((row16 & 3) < count, place, FAR)
    rec_ref[1] = staged[24:40, :]


def there(offset, sign):
    return tuple(
        lax.rem(lax.axis_index(a) + sign * o + lax.axis_size(a), lax.axis_size(a))
        for a, o in zip(AXES, offset)
    )


def greet(devices):
    barrier = pltpu.get_barrier_semaphore()
    for device in devices:
        pl.semaphore_signal(barrier, inc=1, device_id=device, device_id_type=MESH)
    pl.semaphore_wait(barrier, len(devices))


def send(source, target, send_sem, recv_sem, device):
    return pltpu.make_async_remote_copy(
        src_ref=source,
        dst_ref=target,
        send_sem=send_sem,
        recv_sem=recv_sem,
        device_id=device,
        device_id_type=MESH,
    )


def spread_kernel(rec_ref, nbr_ref, send_sem, recv_sem):
    greet([there(d, 1) for d in OFFSETS])
    copies = [
        send(rec_ref, nbr_ref.at[k], send_sem.at[k], recv_sem.at[k], there(d, -1))
        for k, d in enumerate(OFFSETS)
    ]
    for copy in copies:
        copy.start()
    for copy in copies:
        copy.wait()


def turn_kernel(
    fout_ref, fown_ref, x_ref, v_ref, old_ref,
    nbr_ref, new_ref, x2_ref, v2_ref,
    back, send_sem, recv_sem, send2_sem, recv2_sem,
):
    around = {tuple(s * o for o in d) for d in OFFSETS for s in (1, -1)}
    greet([there(d, 1) for d in sorted(around)])
    copies = [
        send(fout_ref.at[k], back.at[k], send_sem.at[k], recv_sem.at[k], there(d, 1))
        for k, d in enumerate(OFFSETS)
    ]
    for copy in copies:
        copy.start()
    for copy in copies:
        copy.wait_recv()
    total = fown_ref[...]
    for k in range(NBR):
        total = total + back[k]
    v = v_ref[...] + HALF_STEP * total
    v = v + HALF_STEP * total
    x = x_ref[...] + TIME_STEP * v
    new_ref[...] = jnp.where(old_ref[0] > 0.1 * FAR, FAR, x)
    again = [
        send(new_ref, nbr_ref.at[k], send2_sem.at[k], recv2_sem.at[k], there(d, -1))
        for k, d in enumerate(OFFSETS)
    ]
    for copy in again:
        copy.start()
    x2_ref[...] = x
    v2_ref[...] = v
    for copy in copies:
        copy.wait_send()
    for copy in again:
        copy.wait()


def last_kernel(
    fout_ref, fown_ref, x_ref, v_ref, rank_ref, xo_ref, vo_ref, fo_ref,
    back, stage, onehot, send_sem, recv_sem,
):
    greet([there(d, -1) for d in OFFSETS])
    copies = [
        send(fout_ref.at[k], back.at[k], send_sem.at[k], recv_sem.at[k], there(d, 1))
        for k, d in enumerate(OFFSETS)
    ]
    for copy in copies:
        copy.start()
    rank = rank_ref[...]
    for t in range(4):
        onehot[TILE * t : TILE * t + TILE, :] = chosen(rank, t)
    for copy in copies:
        copy.wait()
    total = fown_ref[...]
    for k in range(NBR):
        total = total + back[k]
    stage[0:16, :] = x_ref[...]
    stage[12:28, :] = v_ref[...] + HALF_STEP * total
    stage[24:40, :] = total
    stage[36:64, :] = jnp.zeros((28, TILE), F32)
    fields = jnp.concatenate([stage[pl.ds(t, 16, stride=4), :] for t in range(4)], 1)
    out = jnp.dot(split3(fields), onehot[...], preferred_element_type=F32)
    out = (out[32:48] + out[16:32]) + out[0:16]
    xo_ref[...] = out[0:3]
    vo_ref[...] = out[3:6]
    fo_ref[...] = out[6:9]


def call(kernel, outs, scratch, collective=None, ins=None, count=0):
    vmem = pl.BlockSpec(memory_space=pltpu.VMEM)
    params = {"vmem_limit_bytes": 24 << 20}
    if collective is not None:
        params.update(collective_id=collective, has_side_effects=True)
    return pl.pallas_call(
        kernel,
        out_shape=tuple(jax.ShapeDtypeStruct(shape, kind) for shape, kind in outs),
        in_specs=[pl.BlockSpec(memory_space=pltpu.SMEM)] * count + [vmem] * (ins - count),
        out_specs=tuple(vmem for _ in outs),
        scratch_shapes=scratch,
        compiler_params=pltpu.CompilerParams(**params),
    )


def on_device(
    positions, velocities, forces, charges, atom_types, tile_counts, pair_epsilon, pair_sigma
):
    dma = pltpu.SemaphoreType.DMA((NBR,))
    rows = ((16, TILE), F32)
    x, v, rec, rank = call(
        sort_kernel,
        (rows, rows, ((2, 16, TILE), F32), ((4, TILE), jnp.int32)),
        [pltpu.VMEM((64, TILE), F32), pltpu.VMEM((64, TILE), F32)],
        ins=8,
        count=3,
    )(
        tile_counts.reshape(1, 1), pair_epsilon, pair_sigma,
        positions.reshape(12, TILE), velocities.reshape(12, TILE), forces.reshape(12, TILE),
        charges.reshape(4, TILE), atom_types.reshape(4, TILE),
    )
    (first,) = call(
        spread_kernel, (((NBR, 2, 16, TILE), F32),), [dma, dma], collective=0, ins=1
    )(rec)
    fout, fown = pair_forces(first, first, rec, rec, True)
    second, own, x, v = call(
        turn_kernel,
        (((NBR, 16, TILE), F32), rows, rows, rows),
        [pltpu.VMEM((NBR, 16, TILE), F32), dma, dma, dma, dma],
        collective=1,
        ins=5,
    )(fout, fown, x, v, rec)
    fout, fown = pair_forces(second, first, own, rec, False)
    flat = ((3, 4 * TILE), F32)
    outs = call(
        last_kernel,
        (flat, flat, flat),
        [pltpu.VMEM((NBR, 16, TILE), F32), pltpu.VMEM((64, TILE), F32),
         pltpu.VMEM((512, 512), BF16), dma, dma],
        collective=2,
        ins=5,
    )(fout, fown, x, v, rank)
    return tuple(out.reshape(3, 1, 1, 1, 4 * TILE) for out in outs)


def solution(mesh):
    atoms = P(None, "gx", "gy", "gz", None)
    in_specs = (
        atoms, atoms, atoms,
        P("gx", "gy", "gz", None),
        P("gx", "gy", "gz", None),
        P("gx", "gy", "gz"),
        P(), P(),
    )
    return jax.shard_map(
        on_device, mesh=mesh, in_specs=in_specs, out_specs=(atoms,) * 3, check_vma=False
    )
```

```python
import functools

import jax
import jax.numpy as jnp
from jax import lax
from jax.experimental import pallas as pl
from jax.experimental.pallas import tpu as pltpu
from jax.sharding import PartitionSpec as P

TILE = 128
STEPS = 2
TIME_STEP = 0.05
HALF_STEP = 0.025
PLATE = ((1, 0), (1, 1), (0, 1), (-1, 1), (-1, 0), (-1, -1), (0, -1), (1, -1))
NP = len(PLATE)
OFFSETS = tuple((x, y, 0) for x, y in PLATE) + ((0, 0, -1), (0, 0, 1))
NBR = NP + 2
AXES = ("gx", "gy", "gz")
MESH = pl.DeviceIdType.MESH
F32 = jnp.float32
BF16 = jnp.bfloat16
FAR = 1e6
RIGHTS = 4 * (NP + 2)
RROWS = RIGHTS + 8
UNROLL = 4
PAD = 12
LOG2E = 1.4426950408889634
FORCE = 8.0 / (3.24 * 3.24)


def shares(first, pos_ref, par_ref, own_ref, ownpar_ref):
    row = lax.broadcasted_iota(jnp.int32, (64, TILE), 0)
    col = lax.broadcasted_iota(jnp.int32, (64, TILE), 1)
    lane = lax.broadcasted_iota(jnp.int32, (1, TILE), 1) >> 2
    lt, lbox, rt, rbox = row >> 4, (row >> 2) & 3, col & 3, col >> 2
    own_n = ownpar_ref[1, 12:13, :]
    nr = own_n
    for j in range(NP):
        nr = jnp.where(lane == j, par_ref[j, 1, 12:13, :], nr)
    below_n, above_n = par_ref[NP, 1, 12:13, :], par_ref[NP + 1, 1, 12:13, :]
    nl = jnp.where(lbox == 0, below_n, jnp.where(lbox == 2, above_n, own_n))
    nr = jnp.broadcast_to(nr, (64, TILE))
    ahead = (rbox < NP // 2) | ((rbox == NP) & (lbox == 2))
    left_first = (rbox < NP // 2) | ((rbox == NP) & (lbox == 0))
    lf, rf = lt.astype(F32), rt.astype(F32)
    order = jnp.where(left_first, lf * nr + rf, rf * nl + lf)
    if first:
        w1 = jnp.where(left_first, nl, nr)
        w2 = jnp.where(left_first, nr, nl)
    else:
        mine = own_ref[14:15, :]
        below, same, above = mine, mine, mine
        for j in range(NP):
            hit = lane == j
            below = jnp.where(hit, pos_ref[j, 12:13, :], below)
            same = jnp.where(hit, pos_ref[j, 14:15, :], same)
            above = jnp.where(hit, pos_ref[j, 13:14, :], above)
        below = jnp.where(lane == NP, pos_ref[NP, 14:15, :], below)
        above = jnp.where(lane == NP, pos_ref[NP + 1, 14:15, :], above)
        other = jnp.where(lbox == 0, below, jnp.where(lbox == 2, above, same))
        mine = jnp.broadcast_to(mine, (64, TILE))
        w1 = jnp.where(ahead, mine, other)
        w2 = jnp.where(ahead, other, mine)
    w1, w2 = w1 * w1 * w1, w2 * w2 * w2
    inside = (order + 0.5) * (w1 + w2) < w2 * (nl * nr)
    takes = jnp.where(inside, 1.0, 0.0)
    takes = jnp.where(ahead, takes, 1.0 - takes)
    shared = ((rbox < NP) & (lbox < 3)) | ((rbox == NP) & ((lbox == 0) | (lbox == 2)))
    alone = ((rbox == NP) & (lbox == 1) & (lt < rt)) | ((rbox == NP + 1) & (lbox == 1) & (lt == rt))
    return jnp.where(shared, takes, jnp.where(alone, 1.0, 0.0))


def pair_kernel(
    joined, pos_ref, par_ref, own_ref, ownpar_ref, fout_ref, fown_ref,
    left, right, acc_left, acc_right, list_v, list_s, sem,
):
    position = (lambda k: pos_ref[k, 0]) if joined else (lambda k: pos_ref[k])
    own = own_ref[0] if joined else own_ref[...]
    row16 = lax.broadcasted_iota(jnp.int32, (16, 1), 0)
    lane16 = lax.broadcasted_iota(jnp.int32, (1, 16), 1)
    for k in range(NP + 2):
        if k < NP:
            p = position(k) + jnp.where(
                row16 < 4, float(PLATE[k][0]), jnp.where(row16 < 8, float(PLATE[k][1]), 0.0)
            )
            a = par_ref[k, 1]
        else:
            p, a = own, ownpar_ref[1]
        p = p * 2.0
        for f in range(3):
            right[f, 4 * k : 4 * k + 4, :] = p[4 * f : 4 * f + 4]
            right[3 + f, 4 * k : 4 * k + 4, :] = a[4 * f : 4 * f + 4]
    for f in range(6):
        right[f, RIGHTS:RROWS, :] = jnp.full((8, TILE), FAR if f < 3 else 0.0, F32)
    mins, maxs = [], []
    scale = jnp.where(lane16 < 4, 0.04 / 6.0 * FORCE, jnp.where(lane16 < 8, 4.0 * FORCE, 1.0))
    for box in range(3):
        if box == 1:
            p, a = own, ownpar_ref[1]
        else:
            slot = NP if box == 0 else NP + 1
            p = position(slot) + jnp.where(
                (row16 >= 8) & (row16 < 12), -1.0 if box == 0 else 1.0, 0.0
            )
            a = par_ref[slot, 1]
        down = jnp.transpose(jnp.concatenate([p * 2.0, a], 0), (1, 0))
        blocks = down[:, :16].reshape(4, 32, 16)
        mins.append(jnp.min(blocks, axis=1))
        maxs.append(jnp.max(blocks, axis=1))
        scaled = down[:, 16:] * scale
        for t in range(4):
            base = (t * 16 + box * 4) * 4
            for f in range(6):
                at = 4 * (f % 3) + t
                source = down if f < 3 else scaled
                left[f, base : base + 16] = jnp.broadcast_to(
                    source[:, at : at + 1], (TILE, TILE)
                ).reshape(16, 8, TILE)
    for f in range(6):
        left[f, 4 * PAD : 4 * PAD + 4] = jnp.full((4, 8, TILE), FAR if f < 3 else 0.0, F32)
    acc_left[...] = jnp.zeros_like(acc_left)
    acc_right[...] = jnp.zeros_like(acc_right)
    far = jnp.full((4, 16), FAR, F32)
    low = jnp.concatenate(mins + [far], 0)
    high = jnp.concatenate(maxs + [far], 0)
    gaps = jnp.zeros((64, TILE), F32)
    alive = None
    for f in range(3):
        a0 = jnp.concatenate([low[:, 4 * f + t : 4 * f + t + 1] for t in range(4)], 0)
        a1 = jnp.concatenate([high[:, 4 * f + t : 4 * f + t + 1] for t in range(4)], 0)
        v = jnp.concatenate([right[f], jnp.full((TILE - RROWS, TILE), FAR, F32)], 0)
        b0 = jnp.broadcast_to(jnp.min(v, axis=1, keepdims=True), (TILE, TILE))
        b1 = jnp.broadcast_to(jnp.max(v, axis=1, keepdims=True), (TILE, TILE))
        b0 = jnp.transpose(b0, (1, 0))[:1]
        b1 = jnp.transpose(b1, (1, 0))[:1]
        gap = jnp.maximum(jnp.maximum(a0 - b1, b0 - a1), 0.0)
        gaps = gaps + gap * gap
        if f == 0:
            alive = a0 < 0.1 * FAR
    near = (gaps < 3.2401) & alive & (shares(joined, pos_ref, par_ref, own_ref, ownpar_ref) > 0.5)
    row = lax.broadcasted_iota(jnp.int32, (64, TILE), 0)
    r64 = lax.broadcasted_iota(jnp.int32, (64, 64), 0)
    c64 = lax.broadcasted_iota(jnp.int32, (64, 64), 1)
    ones = near.astype(F32)
    before = jnp.dot(
        (c64 < r64).astype(F32).astype(BF16), ones.astype(BF16), preferred_element_type=F32
    )
    place = jnp.where(near, before.astype(jnp.int32), -1)
    lane = lax.broadcasted_iota(jnp.int32, (1, TILE), 1)
    count = jnp.maximum(jnp.sum(ones, axis=0, keepdims=True), 1.0)
    total = jnp.sum(jnp.where(lane < RIGHTS, count, 0.0), axis=1, keepdims=True)
    count = jnp.where(lane < RIGHTS, count, 1e6).astype(jnp.int32)
    value = row - PAD
    for w in range(12):
        word = jnp.zeros((1, TILE), jnp.int32)
        for j in range(4):
            hit = jnp.where(place == 4 * w + j, value, 0)
            word = word + (jnp.sum(hit, axis=0, keepdims=True) + PAD) * (64**j)
        list_v[w : w + 1, :] = word
    list_v[12:13, :] = count
    list_v[13:14, :] = jnp.broadcast_to(total, (1, TILE)).astype(jnp.int32)
    copy = pltpu.make_async_copy(list_v, list_s, sem)
    copy.start()
    copy.wait()

    def turn(_, state):
        r, k = state
        for _ in range(UNROLL):
            b = ((list_s[k >> 2, r] >> ((k & 3) * 6)) & 63) * 4
            at = pl.ds(b, 4)
            rx, ry, rz, rq, re, rs_ = [
                jnp.broadcast_to(right[f, pl.ds(r, 1), :], (8, TILE))[None] for f in range(6)
            ]
            dx = left[0, at] - rx
            dy = left[1, at] - ry
            dz = left[2, at] - rz
            s2 = (dx * dx + 0.09) + dy * dy + dz * dz
            rs = lax.rsqrt(s2)
            inv = rs * rs
            screen = jnp.exp2(s2 * (-LOG2E) * rs)
            w = jnp.maximum(3.33 - s2, 0.0)
            slope = (w * inv) * 1.5
            one = slope + 1.0
            two = one + slope
            size = left[5, at] + rs_
            ratio = size * size * inv
            cubed = ratio * ratio * ratio
            lennard = (left[4, at] * re) * cubed * (cubed * two - one)
            coulomb = (left[3, at] * rq) * screen * (rs * (one + 5.0) + slope)
            g = (lennard + coulomb) * w
            fx, fy, fz = g * dx, g * dy, g * dz
            acc_left[0, at] += fx
            acc_left[1, at] += fy
            acc_left[2, at] += fz
            acc_right[0, r] -= jnp.sum(fx, axis=0)
            acc_right[1, r] -= jnp.sum(fy, axis=0)
            acc_right[2, r] -= jnp.sum(fz, axis=0)
            on = k + 1 >= list_s[12, r]
            k = jnp.where(on, 0, k + 1)
            r = jnp.where(on, r + 1, r)
        return r, k

    lax.fori_loop(0, (list_s[13, 0] + UNROLL - 1) // UNROLL, turn, (jnp.int32(0), jnp.int32(0)))
    plate = par_ref[0, 1, 12:13, :]
    for k in range(1, NP):
        plate = plate + par_ref[k, 1, 12:13, :]
    tower = ownpar_ref[1, 12:13, :] + par_ref[NP, 1, 12:13, :] + par_ref[NP + 1, 1, 12:13, :]
    tail = jnp.broadcast_to(plate * tower, (4, TILE))

    def gathered(k):
        rows = [jnp.sum(acc_right[f, 4 * k : 4 * k + 4], axis=1) for f in range(3)]
        return jnp.concatenate(rows + [tail], 0)

    for k in range(NP):
        fout_ref[k] = gathered(k)
    unit = jnp.ones((8, TILE), BF16)
    for box in range(3):
        rows = []
        for f in range(3):
            for t in range(4):
                base = (t * 16 + box * 4) * 4
                a = acc_left[f, base : base + 16].reshape(TILE, TILE)
                hi = a.astype(BF16)
                lo = (a - hi.astype(F32)).astype(BF16)
                dims = (((1,), (1,)), ((), ()))
                v = lax.dot_general(unit, hi, dims, preferred_element_type=F32)
                v = v + lax.dot_general(unit, lo, dims, preferred_element_type=F32)
                rows.append(v[:1])
        out = jnp.concatenate(rows + [tail], 0)
        if box == 1:
            fown_ref[0:12, :] = (out + gathered(NP))[0:12]
            fown_ref[12:16, :] = tail
        else:
            fout_ref[NP if box == 0 else NP + 1] = out


def pair_forces(pos, par, own, ownpar, joined):
    vmem = pl.BlockSpec(memory_space=pltpu.VMEM)
    return pl.pallas_call(
        functools.partial(pair_kernel, joined),
        out_shape=(
            jax.ShapeDtypeStruct((NBR, 16, TILE), F32),
            jax.ShapeDtypeStruct((16, TILE), F32),
        ),
        in_specs=[vmem] * 4,
        out_specs=(vmem, vmem),
        scratch_shapes=[
            pltpu.VMEM((6, 256, 8, TILE), F32),
            pltpu.VMEM((6, RROWS, TILE), F32),
            pltpu.VMEM((3, 256, 8, TILE), F32),
            pltpu.VMEM((3, RROWS, 8, TILE), F32),
            pltpu.VMEM((16, TILE), jnp.int32),
            pltpu.SMEM((16, TILE), jnp.int32),
            pltpu.SemaphoreType.DMA,
        ],
        compiler_params=pltpu.CompilerParams(vmem_limit_bytes=24 << 20),
    )(pos, par, own, ownpar)


def hilbert(cells, bits):
    x = list(cells)
    q = 1 << (bits - 1)
    while q > 1:
        p = q - 1
        for i in range(3):
            hit = (x[i] & q) != 0
            if i == 0:
                x[0] = jnp.where(hit, x[0] ^ p, x[0])
            else:
                swap = (x[0] ^ x[i]) & p
                x[0], x[i] = jnp.where(hit, x[0] ^ p, x[0] ^ swap), jnp.where(hit, x[i], x[i] ^ swap)
        q >>= 1
    x[1] = x[1] ^ x[0]
    x[2] = x[2] ^ x[1]
    flip = jnp.zeros_like(x[0])
    q = 1 << (bits - 1)
    while q > 1:
        flip = jnp.where((x[2] & q) != 0, flip ^ (q - 1), flip)
        q >>= 1
    x = [v ^ flip for v in x]
    key = jnp.zeros_like(x[0])
    for bit in range(bits - 1, -1, -1):
        for a in range(3):
            key = key * 2 + ((x[a] >> bit) & 1)
    return key


def split3(a):
    hi = a.astype(BF16)
    rest = a - hi.astype(F32)
    mid = rest.astype(BF16)
    lo = (rest - mid.astype(F32)).astype(BF16)
    return jnp.concatenate([hi, mid, lo], 0)


def chosen(rank, t):
    place = lax.broadcasted_iota(jnp.int32, (TILE, TILE), 0) + TILE * t
    tiles = [(rank[j : j + 1, :] == place).astype(F32).astype(BF16) for j in range(4)]
    return jnp.concatenate(tiles, 1)


def sort_kernel(*refs):
    given, (x_ref, v_ref, rec_ref, rank_ref), held = refs[:8], refs[8:12], refs[12:20]
    stage, staged, sem = refs[20:]
    copies = [
        pltpu.make_async_copy(source, target, sem.at[i])
        for i, (source, target) in enumerate(zip(given, held))
    ]
    for copy in copies:
        copy.start()
    for copy in copies:
        copy.wait()
    pos_ref, vel_ref, frc_ref, chg_ref, typ_ref, count_ref, eps_ref, sig_ref = held

    def rows(ref, f):
        return [ref[f, 0, 0, :, TILE * t : TILE * t + TILE] for t in range(4)]

    def rows1(ref):
        return [ref[0, 0, :, TILE * t : TILE * t + TILE] for t in range(4)]

    def flat(ref):
        return jnp.concatenate([row for f in range(3) for row in rows(ref, f)], 0)

    v = flat(vel_ref) + HALF_STEP * flat(frc_ref)
    x = flat(pos_ref) + TIME_STEP * v
    count = count_ref[0, 0, 0]
    row = lax.broadcasted_iota(jnp.int32, (4, TILE), 0)
    live = row < count
    kinds = jnp.concatenate(rows1(typ_ref), 0)
    eps = jnp.zeros((4, TILE), F32)
    sig = jnp.zeros((4, TILE), F32)
    for k in range(eps_ref.shape[0]):
        eps = jnp.where(kinds == k, eps_ref[k], eps)
        sig = jnp.where(kinds == k, sig_ref[k], sig)
    alive = live.astype(F32)
    stage[...] = jnp.zeros_like(stage)
    stage[0:12, :] = x
    stage[12:24, :] = v
    stage[24:28, :] = jnp.concatenate(rows1(chg_ref), 0) * alive
    stage[28:32, :] = jnp.sqrt(eps) * alive
    stage[32:36, :] = sig
    cells = [
        jnp.clip((jnp.clip(x[4 * a : 4 * a + 4], -1.0, 2.0) * 4.0).astype(jnp.int32), 0, 3)
        for a in range(3)
    ]
    index = row * TILE + lax.broadcasted_iota(jnp.int32, (4, TILE), 1)
    key = jnp.where(live, hilbert(cells, 2), 64) * 512 + index
    key = jnp.concatenate([key.astype(F32), jnp.zeros((4, TILE), F32)], 0)
    down = jnp.transpose(key, (1, 0))
    ranks = []
    for j in range(4):
        less = jnp.zeros((TILE, TILE), F32)
        for i in range(4):
            less = less + (down[:, i : i + 1] < key[j : j + 1, :]).astype(F32)
        ranks.append(jnp.sum(less, axis=0, keepdims=True))
    rank = jnp.concatenate(ranks, 0).astype(jnp.int32)
    rank_ref[...] = rank
    fields = jnp.concatenate([stage[pl.ds(t, 16, stride=4), :] for t in range(4)], 1)
    parts = split3(fields)
    for t in range(4):
        out = lax.dot_general(
            parts, chosen(rank, t), (((1,), (1,)), ((), ())), preferred_element_type=F32
        )
        staged[pl.ds(t, 16, stride=4), :] = (out[32:48] + out[16:32]) + out[0:16]
    row16 = lax.broadcasted_iota(jnp.int32, (16, TILE), 0)
    place = staged[0:16, :]
    x_ref[...] = place
    v_ref[...] = staged[12:28, :]
    rec_ref[0] = jnp.where((row16 & 3) < count, place, FAR)
    rec_ref[1] = jnp.where(row16 < 12, staged[24:40, :], count.astype(F32))


def there(offset, sign):
    return tuple(
        lax.rem(lax.axis_index(a) + sign * o + lax.axis_size(a), lax.axis_size(a))
        for a, o in zip(AXES, offset)
    )


def greet(devices):
    barrier = pltpu.get_barrier_semaphore()
    for device in devices:
        pl.semaphore_signal(barrier, inc=1, device_id=device, device_id_type=MESH)
    pl.semaphore_wait(barrier, len(devices))


def send(source, target, send_sem, recv_sem, device):
    return pltpu.make_async_remote_copy(
        src_ref=source,
        dst_ref=target,
        send_sem=send_sem,
        recv_sem=recv_sem,
        device_id=device,
        device_id_type=MESH,
    )


def spread_kernel(rec_ref, nbr_ref, send_sem, recv_sem):
    greet([there(d, 1) for d in OFFSETS])
    copies = [
        send(rec_ref, nbr_ref.at[k], send_sem.at[k], recv_sem.at[k], there(d, -1))
        for k, d in enumerate(OFFSETS)
    ]
    for copy in copies:
        copy.start()
    for copy in copies:
        copy.wait()


def turn_kernel(
    fout_ref, fown_ref, x_ref, v_ref, old_ref,
    nbr_ref, new_ref, x2_ref, v2_ref,
    back, send_sem, recv_sem, send2_sem, recv2_sem,
):
    greet([there(d, 1) for d in OFFSETS])
    copies = [
        send(fout_ref.at[k], back.at[k], send_sem.at[k], recv_sem.at[k], there(d, 1))
        for k, d in enumerate(OFFSETS)
    ]
    for copy in copies:
        copy.start()
    for copy in copies:
        copy.wait_recv()
    total = fown_ref[...]
    for k in range(NBR):
        total = total + back[k]
    v = v_ref[...] + HALF_STEP * total
    v = v + HALF_STEP * total
    x = x_ref[...] + TIME_STEP * v
    row16 = lax.broadcasted_iota(jnp.int32, (16, TILE), 0)
    new = jnp.where(old_ref[0] > 0.1 * FAR, FAR, x)
    new = jnp.where(row16 == 12, back[NP + 1, 12:13, :], new)
    new = jnp.where(row16 == 13, back[NP, 12:13, :], new)
    new_ref[...] = jnp.where(row16 == 14, fown_ref[12:13, :], new)
    again = [
        send(new_ref, nbr_ref.at[k], send2_sem.at[k], recv2_sem.at[k], there(d, -1))
        for k, d in enumerate(OFFSETS)
    ]
    for copy in again:
        copy.start()
    x2_ref[...] = x
    v2_ref[...] = v
    for copy in copies:
        copy.wait_send()
    for copy in again:
        copy.wait()


def last_kernel(
    fout_ref, fown_ref, x_ref, v_ref, rank_ref, xo_ref, vo_ref, fo_ref,
    back, stage, onehot, send_sem, recv_sem,
):
    greet([there(d, -1) for d in OFFSETS])
    copies = [
        send(fout_ref.at[k], back.at[k], send_sem.at[k], recv_sem.at[k], there(d, 1))
        for k, d in enumerate(OFFSETS)
    ]
    for copy in copies:
        copy.start()
    rank = rank_ref[...]
    for t in range(4):
        onehot[TILE * t : TILE * t + TILE, :] = chosen(rank, t)
    for copy in copies:
        copy.wait()
    total = fown_ref[...]
    for k in range(NBR):
        total = total + back[k]
    stage[0:16, :] = x_ref[...]
    stage[12:28, :] = v_ref[...] + HALF_STEP * total
    stage[24:40, :] = total
    stage[36:64, :] = jnp.zeros((28, TILE), F32)
    fields = jnp.concatenate([stage[pl.ds(t, 16, stride=4), :] for t in range(4)], 1)
    out = jnp.dot(split3(fields), onehot[...], preferred_element_type=F32)
    out = (out[32:48] + out[16:32]) + out[0:16]
    for f in range(3):
        xo_ref[f, 0, 0] = out[f : f + 1]
        vo_ref[f, 0, 0] = out[3 + f : 4 + f]
        fo_ref[f, 0, 0] = out[6 + f : 7 + f]


def place_kernel(*refs):
    copies = [pltpu.make_async_copy(refs[i], refs[3 + i], refs[6].at[i]) for i in range(3)]
    for copy in copies:
        copy.start()
    for copy in copies:
        copy.wait()


def call(kernel, outs, scratch, collective=None, ins=None, raw_in=False, raw_out=False, limit=24 << 20):
    vmem = pl.BlockSpec(memory_space=pltpu.VMEM)
    hbm = pl.BlockSpec(memory_space=pltpu.HBM)
    params = {"vmem_limit_bytes": limit}
    if collective is not None:
        params.update(collective_id=collective, has_side_effects=True)
    return pl.pallas_call(
        kernel,
        out_shape=tuple(jax.ShapeDtypeStruct(shape, kind) for shape, kind in outs),
        in_specs=[hbm if raw_in else vmem] * ins,
        out_specs=tuple(hbm if raw_out else vmem for _ in outs),
        scratch_shapes=scratch,
        compiler_params=pltpu.CompilerParams(**params),
    )


def on_device(
    positions, velocities, forces, charges, atom_types, tile_counts, pair_epsilon, pair_sigma
):
    dma = pltpu.SemaphoreType.DMA((NBR,))
    rows = ((16, TILE), F32)
    wide = (positions, velocities, forces, charges, atom_types)
    small = (tile_counts, pair_epsilon, pair_sigma)
    x, v, rec, rank = call(
        sort_kernel,
        (rows, rows, ((2, 16, TILE), F32), ((4, TILE), jnp.int32)),
        [pltpu.VMEM(given.shape, given.dtype) for given in wide]
        + [pltpu.SMEM(given.shape, given.dtype) for given in small]
        + [pltpu.VMEM((64, TILE), F32), pltpu.VMEM((64, TILE), F32), pltpu.SemaphoreType.DMA((8,))],
        ins=8,
        raw_in=True,
        limit=67043328,
    )(
        *wide, *small
    )
    (first,) = call(
        spread_kernel, (((NBR, 2, 16, TILE), F32),), [dma, dma], collective=0, ins=1
    )(rec)
    fout, fown = pair_forces(first, first, rec, rec, True)
    second, own, x, v = call(
        turn_kernel,
        (((NBR, 16, TILE), F32), rows, rows, rows),
        [pltpu.VMEM((NBR, 16, TILE), F32), dma, dma, dma, dma],
        collective=1,
        ins=5,
    )(fout, fown, x, v, rec)
    fout, fown = pair_forces(second, first, own, rec, False)
    flat = ((3, 1, 1, 1, 4 * TILE), F32)
    outs = call(
        last_kernel,
        (flat, flat, flat),
        [pltpu.VMEM((NBR, 16, TILE), F32), pltpu.VMEM((64, TILE), F32),
         pltpu.VMEM((512, 512), BF16), dma, dma],
        collective=2,
        ins=5,
    )(fout, fown, x, v, rank)
    return call(
        place_kernel, (flat, flat, flat), [pltpu.SemaphoreType.DMA((3,))], ins=3, raw_out=True
    )(*outs)


def solution(mesh):
    atoms = P(None, "gx", "gy", "gz", None)
    in_specs = (
        atoms, atoms, atoms,
        P("gx", "gy", "gz", None),
        P("gx", "gy", "gz", None),
        P("gx", "gy", "gz"),
        P(), P(),
    )
    return jax.shard_map(
        on_device, mesh=mesh, in_specs=in_specs, out_specs=(atoms,) * 3, check_vma=False
    )
```

```python
import functools

import jax
import jax.numpy as jnp
from jax import lax
from jax.experimental import pallas as pl
from jax.experimental.pallas import tpu as pltpu
from jax.sharding import PartitionSpec as P

TILE = 128
STEPS = 2
TIME_STEP = 0.05
HALF_STEP = 0.025
PLATE = ((1, 0), (1, 1), (0, 1), (-1, 1), (-1, 0), (-1, -1), (0, -1), (1, -1))
NP = len(PLATE)
OFFSETS = tuple((x, y, 0) for x, y in PLATE) + ((0, 0, -1), (0, 0, 1))
NBR = NP + 2
AXES = ("gx", "gy", "gz")
MESH = pl.DeviceIdType.MESH
F32 = jnp.float32
BF16 = jnp.bfloat16
FAR = 1e6
RIGHTS = 4 * (NP + 2)
RROWS = RIGHTS + 8
UNROLL = 8
PAD = 12
LOG2E = 1.4426950408889634
FORCE = 8.0 / (3.24 * 3.24)


def shares(first, pos_ref, par_ref, own_ref, ownpar_ref):
    row = lax.broadcasted_iota(jnp.int32, (64, TILE), 0)
    col = lax.broadcasted_iota(jnp.int32, (64, TILE), 1)
    lane = lax.broadcasted_iota(jnp.int32, (1, TILE), 1) >> 2
    lt, lbox, rt, rbox = row >> 4, (row >> 2) & 3, col & 3, col >> 2
    own_n = ownpar_ref[1, 12:13, :]
    nr = own_n
    for j in range(NP):
        nr = jnp.where(lane == j, par_ref[j, 1, 12:13, :], nr)
    below_n, above_n = par_ref[NP, 1, 12:13, :], par_ref[NP + 1, 1, 12:13, :]
    nl = jnp.where(lbox == 0, below_n, jnp.where(lbox == 2, above_n, own_n))
    nr = jnp.broadcast_to(nr, (64, TILE))
    ahead = (rbox < NP // 2) | ((rbox == NP) & (lbox == 2))
    left_first = (rbox < NP // 2) | ((rbox == NP) & (lbox == 0))
    lf, rf = lt.astype(F32), rt.astype(F32)
    order = jnp.where(left_first, lf * nr + rf, rf * nl + lf)
    if first:
        w1 = jnp.where(left_first, nl, nr)
        w2 = jnp.where(left_first, nr, nl)
    else:
        mine = own_ref[14:15, :]
        below, same, above = mine, mine, mine
        for j in range(NP):
            hit = lane == j
            below = jnp.where(hit, pos_ref[j, 12:13, :], below)
            same = jnp.where(hit, pos_ref[j, 14:15, :], same)
            above = jnp.where(hit, pos_ref[j, 13:14, :], above)
        below = jnp.where(lane == NP, pos_ref[NP, 14:15, :], below)
        above = jnp.where(lane == NP, pos_ref[NP + 1, 14:15, :], above)
        other = jnp.where(lbox == 0, below, jnp.where(lbox == 2, above, same))
        mine = jnp.broadcast_to(mine, (64, TILE))
        w1 = jnp.where(ahead, mine, other)
        w2 = jnp.where(ahead, other, mine)
    w1, w2 = w1 * w1 * w1, w2 * w2 * w2
    inside = (order + 0.5) * (w1 + w2) < w2 * (nl * nr)
    takes = jnp.where(inside, 1.0, 0.0)
    takes = jnp.where(ahead, takes, 1.0 - takes)
    shared = ((rbox < NP) & (lbox < 3)) | ((rbox == NP) & ((lbox == 0) | (lbox == 2)))
    alone = ((rbox == NP) & (lbox == 1) & (lt < rt)) | ((rbox == NP + 1) & (lbox == 1) & (lt == rt))
    return jnp.where(shared, takes, jnp.where(alone, 1.0, -1.0))


def pair_kernel(
    joined, pos_ref, par_ref, own_ref, ownpar_ref, fout_ref, fown_ref,
    left, right, acc_left, acc_right, list_v, list_s, sem,
):
    position = (lambda k: pos_ref[k, 0]) if joined else (lambda k: pos_ref[k])
    own = own_ref[0] if joined else own_ref[...]
    row16 = lax.broadcasted_iota(jnp.int32, (16, 1), 0)
    lane16 = lax.broadcasted_iota(jnp.int32, (1, 16), 1)
    for k in range(NP + 2):
        if k < NP:
            p = position(k) + jnp.where(
                row16 < 4, float(PLATE[k][0]), jnp.where(row16 < 8, float(PLATE[k][1]), 0.0)
            )
            a = par_ref[k, 1]
        else:
            p, a = own, ownpar_ref[1]
        p = p * 2.0
        for f in range(3):
            right[f, 4 * k : 4 * k + 4, :] = p[4 * f : 4 * f + 4]
            right[3 + f, 4 * k : 4 * k + 4, :] = a[4 * f : 4 * f + 4]
    for f in range(6):
        right[f, RIGHTS:RROWS, :] = jnp.full((8, TILE), FAR if f < 3 else 0.0, F32)
    mins, maxs, downs = [], [], []
    scale = jnp.where(lane16 < 4, 0.04 / 6.0 * FORCE, jnp.where(lane16 < 8, 4.0 * FORCE, 1.0))
    for box in range(3):
        if box == 1:
            p, a = own, ownpar_ref[1]
        else:
            slot = NP if box == 0 else NP + 1
            p = position(slot) + jnp.where(
                (row16 >= 8) & (row16 < 12), -1.0 if box == 0 else 1.0, 0.0
            )
            a = par_ref[slot, 1]
        down = jnp.transpose(jnp.concatenate([p * 2.0, a], 0), (1, 0))
        blocks = down[:, :16].reshape(4, 32, 16)
        mins.append(jnp.min(blocks, axis=1))
        maxs.append(jnp.max(blocks, axis=1))
        downs.append(down)
    far = jnp.full((4, 16), FAR, F32)
    low = jnp.concatenate(mins + [far], 0)
    high = jnp.concatenate(maxs + [far], 0)
    gaps = jnp.zeros((64, TILE), F32)
    alive = None
    for f in range(3):
        a0 = jnp.concatenate([low[:, 4 * f + t : 4 * f + t + 1] for t in range(4)], 0)
        a1 = jnp.concatenate([high[:, 4 * f + t : 4 * f + t + 1] for t in range(4)], 0)
        v = jnp.concatenate([right[f], jnp.full((TILE - RROWS, TILE), FAR, F32)], 0)
        b0 = jnp.broadcast_to(jnp.min(v, axis=1, keepdims=True), (TILE, TILE))
        b1 = jnp.broadcast_to(jnp.max(v, axis=1, keepdims=True), (TILE, TILE))
        b0 = jnp.transpose(b0, (1, 0))[:1]
        b1 = jnp.transpose(b1, (1, 0))[:1]
        gap = jnp.maximum(jnp.maximum(a0 - b1, b0 - a1), 0.0)
        gaps = gaps + gap * gap
        if f == 0:
            alive = a0 < 0.1 * FAR
    mine = shares(joined, pos_ref, par_ref, own_ref, ownpar_ref)
    close = (gaps < 3.2401) & alive
    near = close & (mine > 0.5)
    weight = jnp.sum(jnp.where(close & (mine > -0.5), 1.0, 0.0), axis=0, keepdims=True)
    weight = jnp.sum(weight, axis=1, keepdims=True) + 1.0
    row = lax.broadcasted_iota(jnp.int32, (64, TILE), 0)
    r64 = lax.broadcasted_iota(jnp.int32, (64, 64), 0)
    c64 = lax.broadcasted_iota(jnp.int32, (64, 64), 1)
    ones = near.astype(F32)
    before = jnp.dot(
        (c64 < r64).astype(F32).astype(BF16), ones.astype(BF16), preferred_element_type=F32
    )
    place = jnp.where(near, before.astype(jnp.int32), -1)
    lane = lax.broadcasted_iota(jnp.int32, (1, TILE), 1)
    count = jnp.maximum(jnp.sum(ones, axis=0, keepdims=True), 1.0)
    total = jnp.sum(jnp.where(lane < RIGHTS, count, 0.0), axis=1, keepdims=True)
    count = jnp.where(lane < RIGHTS, count, 1e6).astype(jnp.int32)
    value = row - PAD
    for w in range(12):
        word = jnp.zeros((1, TILE), jnp.int32)
        for j in range(4):
            hit = jnp.where(place == 4 * w + j, value, 0)
            word = word + (jnp.sum(hit, axis=0, keepdims=True) + PAD) * (64**j)
        list_v[w : w + 1, :] = word
    list_v[12:13, :] = count
    list_v[13:14, :] = jnp.broadcast_to(total, (1, TILE)).astype(jnp.int32)
    copy = pltpu.make_async_copy(list_v, list_s, sem)
    copy.start()
    for box, down in enumerate(downs):
        scaled = down[:, 16:] * scale
        for t in range(4):
            base = (t * 16 + box * 4) * 4
            for f in range(6):
                at = 4 * (f % 3) + t
                source = down if f < 3 else scaled
                left[f, base : base + 16] = jnp.broadcast_to(
                    source[:, at : at + 1], (TILE, TILE)
                ).reshape(16, 8, TILE)
    for f in range(6):
        left[f, 4 * PAD : 4 * PAD + 4] = jnp.full((4, 8, TILE), FAR if f < 3 else 0.0, F32)
    acc_left[...] = jnp.zeros_like(acc_left)
    acc_right[...] = jnp.zeros_like(acc_right)
    copy.wait()

    def turn(_, state):
        r, k = state
        for _ in range(UNROLL):
            b = ((list_s[k >> 2, r] >> ((k & 3) * 6)) & 63) * 4
            at = pl.ds(b, 4)
            rx, ry, rz, rq, re, rs_ = [
                jnp.broadcast_to(right[f, pl.ds(r, 1), :], (8, TILE))[None] for f in range(6)
            ]
            dx = left[0, at] - rx
            dy = left[1, at] - ry
            dz = left[2, at] - rz
            s2 = (dx * dx + 0.09) + dy * dy + dz * dz
            rs = lax.rsqrt(s2)
            inv = rs * rs
            screen = jnp.exp2(s2 * (-LOG2E) * rs)
            w = jnp.maximum(3.33 - s2, 0.0)
            slope = (w * inv) * 1.5
            one = slope + 1.0
            two = one + slope
            size = left[5, at] + rs_
            ratio = size * size * inv
            cubed = ratio * ratio * ratio
            lennard = (left[4, at] * re) * cubed * (cubed * two - one)
            coulomb = (left[3, at] * rq) * screen * (rs * (one + 5.0) + slope)
            g = (lennard + coulomb) * w
            fx, fy, fz = g * dx, g * dy, g * dz
            acc_left[0, at] += fx
            acc_left[1, at] += fy
            acc_left[2, at] += fz
            acc_right[0, r] -= jnp.sum(fx, axis=0)
            acc_right[1, r] -= jnp.sum(fy, axis=0)
            acc_right[2, r] -= jnp.sum(fz, axis=0)
            on = k + 1 >= list_s[12, r]
            k = jnp.where(on, 0, k + 1)
            r = jnp.where(on, r + 1, r)
        return r, k

    lax.fori_loop(0, (list_s[13, 0] + UNROLL - 1) // UNROLL, turn, (jnp.int32(0), jnp.int32(0)))
    tail = jnp.broadcast_to(weight, (4, TILE))

    def gathered(k):
        rows = [jnp.sum(acc_right[f, 4 * k : 4 * k + 4], axis=1) for f in range(3)]
        return jnp.concatenate(rows + [tail], 0)

    for k in range(NP):
        fout_ref[k] = gathered(k)
    ones = [
        jnp.where(lax.broadcasted_iota(jnp.int32, (2 * TILE, TILE), 1) == f, 1.0, 0.0).astype(BF16)
        for f in range(3)
    ]
    ones = jnp.concatenate(ones, 0)
    for box in range(3):
        parts = []
        for t in range(4):
            base = (t * 16 + box * 4) * 4
            halves = []
            for f in range(3):
                a = acc_left[f, base : base + 16].reshape(TILE, TILE)
                hi = a.astype(BF16)
                halves += [hi, (a - hi.astype(F32)).astype(BF16)]
            parts.append(jnp.concatenate(halves, 1))
        sums = jnp.dot(jnp.concatenate(parts, 0), ones, preferred_element_type=F32)
        target = fown_ref if box == 1 else fout_ref.at[NP if box == 0 else NP + 1]
        other = gathered(NP)
        for t in range(4):
            row = jnp.transpose(sums[TILE * t : TILE * t + TILE], (1, 0))
            for f in range(3):
                at = 4 * f + t
                value = row[f : f + 1]
                target[at : at + 1, :] = value + other[at : at + 1] if box == 1 else value
        target[12:16, :] = tail


def pair_forces(pos, par, own, ownpar, joined):
    vmem = pl.BlockSpec(memory_space=pltpu.VMEM)
    return pl.pallas_call(
        functools.partial(pair_kernel, joined),
        out_shape=(
            jax.ShapeDtypeStruct((NBR, 16, TILE), F32),
            jax.ShapeDtypeStruct((16, TILE), F32),
        ),
        in_specs=[vmem] * 4,
        out_specs=(vmem, vmem),
        scratch_shapes=[
            pltpu.VMEM((6, 256, 8, TILE), F32),
            pltpu.VMEM((6, RROWS, TILE), F32),
            pltpu.VMEM((3, 256, 8, TILE), F32),
            pltpu.VMEM((3, RROWS, 8, TILE), F32),
            pltpu.VMEM((16, TILE), jnp.int32),
            pltpu.SMEM((16, TILE), jnp.int32),
            pltpu.SemaphoreType.DMA,
        ],
        compiler_params=pltpu.CompilerParams(vmem_limit_bytes=24 << 20),
    )(pos, par, own, ownpar)


def hilbert(cells, bits):
    x = list(cells)
    q = 1 << (bits - 1)
    while q > 1:
        p = q - 1
        for i in range(3):
            hit = (x[i] & q) != 0
            if i == 0:
                x[0] = jnp.where(hit, x[0] ^ p, x[0])
            else:
                swap = (x[0] ^ x[i]) & p
                x[0], x[i] = jnp.where(hit, x[0] ^ p, x[0] ^ swap), jnp.where(hit, x[i], x[i] ^ swap)
        q >>= 1
    x[1] = x[1] ^ x[0]
    x[2] = x[2] ^ x[1]
    flip = jnp.zeros_like(x[0])
    q = 1 << (bits - 1)
    while q > 1:
        flip = jnp.where((x[2] & q) != 0, flip ^ (q - 1), flip)
        q >>= 1
    x = [v ^ flip for v in x]
    key = jnp.zeros_like(x[0])
    for bit in range(bits - 1, -1, -1):
        for a in range(3):
            key = key * 2 + ((x[a] >> bit) & 1)
    return key


def split3(a):
    hi = a.astype(BF16)
    rest = a - hi.astype(F32)
    mid = rest.astype(BF16)
    lo = (rest - mid.astype(F32)).astype(BF16)
    return jnp.concatenate([hi, mid, lo], 0)


def chosen(rank, t):
    place = lax.broadcasted_iota(jnp.int32, (TILE, TILE), 0) + TILE * t
    tiles = [(rank[j : j + 1, :] == place).astype(F32).astype(BF16) for j in range(4)]
    return jnp.concatenate(tiles, 1)


def sort_kernel(*refs):
    given, (x_ref, v_ref, rec_ref, rank_ref), held = refs[:8], refs[8:12], refs[12:20]
    stage, staged, sem = refs[20:]
    copies = [
        pltpu.make_async_copy(source, target, sem.at[i])
        for i, (source, target) in enumerate(zip(given, held))
    ]
    for copy in copies:
        copy.start()
    for copy in copies:
        copy.wait()
    pos_ref, vel_ref, frc_ref, chg_ref, typ_ref, count_ref, eps_ref, sig_ref = held

    def rows(ref, f):
        return [ref[f, 0, 0, :, TILE * t : TILE * t + TILE] for t in range(4)]

    def rows1(ref):
        return [ref[0, 0, :, TILE * t : TILE * t + TILE] for t in range(4)]

    def flat(ref):
        return jnp.concatenate([row for f in range(3) for row in rows(ref, f)], 0)

    v = flat(vel_ref) + HALF_STEP * flat(frc_ref)
    x = flat(pos_ref) + TIME_STEP * v
    count = count_ref[0, 0, 0]
    row = lax.broadcasted_iota(jnp.int32, (4, TILE), 0)
    live = row < count
    kinds = jnp.concatenate(rows1(typ_ref), 0)
    eps = jnp.zeros((4, TILE), F32)
    sig = jnp.zeros((4, TILE), F32)
    for k in range(eps_ref.shape[0]):
        eps = jnp.where(kinds == k, eps_ref[k], eps)
        sig = jnp.where(kinds == k, sig_ref[k], sig)
    alive = live.astype(F32)
    stage[...] = jnp.zeros_like(stage)
    stage[0:12, :] = x
    stage[12:24, :] = v
    stage[24:28, :] = jnp.concatenate(rows1(chg_ref), 0) * alive
    stage[28:32, :] = jnp.sqrt(eps) * alive
    stage[32:36, :] = sig
    cells = [
        jnp.clip((jnp.clip(x[4 * a : 4 * a + 4], -1.0, 2.0) * 4.0).astype(jnp.int32), 0, 3)
        for a in range(3)
    ]
    index = row * TILE + lax.broadcasted_iota(jnp.int32, (4, TILE), 1)
    key = jnp.where(live, hilbert(cells, 2), 64) * 512 + index
    key = jnp.concatenate([key.astype(F32), jnp.zeros((4, TILE), F32)], 0)
    down = jnp.transpose(key, (1, 0))
    ranks = []
    for j in range(4):
        less = jnp.zeros((TILE, TILE), F32)
        for i in range(4):
            less = less + (down[:, i : i + 1] < key[j : j + 1, :]).astype(F32)
        ranks.append(jnp.sum(less, axis=0, keepdims=True))
    rank = jnp.concatenate(ranks, 0).astype(jnp.int32)
    rank_ref[...] = rank
    fields = jnp.concatenate([stage[pl.ds(t, 16, stride=4), :] for t in range(4)], 1)
    parts = split3(fields)
    for t in range(4):
        out = lax.dot_general(
            parts, chosen(rank, t), (((1,), (1,)), ((), ())), preferred_element_type=F32
        )
        staged[pl.ds(t, 16, stride=4), :] = (out[32:48] + out[16:32]) + out[0:16]
    row16 = lax.broadcasted_iota(jnp.int32, (16, TILE), 0)
    place = staged[0:16, :]
    x_ref[...] = place
    v_ref[...] = staged[12:28, :]
    rec_ref[0] = jnp.where((row16 & 3) < count, place, FAR)
    rec_ref[1] = jnp.where(row16 < 12, staged[24:40, :], count.astype(F32))


def there(offset, sign):
    return tuple(
        lax.rem(lax.axis_index(a) + sign * o + lax.axis_size(a), lax.axis_size(a))
        for a, o in zip(AXES, offset)
    )


def greet(devices):
    barrier = pltpu.get_barrier_semaphore()
    for device in devices:
        pl.semaphore_signal(barrier, inc=1, device_id=device, device_id_type=MESH)
    pl.semaphore_wait(barrier, len(devices))


def send(source, target, send_sem, recv_sem, device):
    return pltpu.make_async_remote_copy(
        src_ref=source,
        dst_ref=target,
        send_sem=send_sem,
        recv_sem=recv_sem,
        device_id=device,
        device_id_type=MESH,
    )


def spread_kernel(rec_ref, nbr_ref, send_sem, recv_sem):
    greet([there(d, 1) for d in OFFSETS])
    copies = [
        send(rec_ref, nbr_ref.at[k], send_sem.at[k], recv_sem.at[k], there(d, -1))
        for k, d in enumerate(OFFSETS)
    ]
    for copy in copies:
        copy.start()
    for copy in copies:
        copy.wait()


def turn_kernel(
    fout_ref, fown_ref, x_ref, v_ref, old_ref,
    nbr_ref, new_ref, x2_ref, v2_ref,
    back, send_sem, recv_sem, send2_sem, recv2_sem,
):
    greet([there(d, 1) for d in OFFSETS])
    copies = [
        send(fout_ref.at[k], back.at[k], send_sem.at[k], recv_sem.at[k], there(d, 1))
        for k, d in enumerate(OFFSETS)
    ]
    for copy in copies:
        copy.start()
    for copy in copies:
        copy.wait_recv()
    total = fown_ref[...]
    for k in range(NBR):
        total = total + back[k]
    v = v_ref[...] + HALF_STEP * total
    v = v + HALF_STEP * total
    x = x_ref[...] + TIME_STEP * v
    row16 = lax.broadcasted_iota(jnp.int32, (16, TILE), 0)
    new = jnp.where(old_ref[0] > 0.1 * FAR, FAR, x)
    new = jnp.where(row16 == 12, back[NP + 1, 12:13, :], new)
    new = jnp.where(row16 == 13, back[NP, 12:13, :], new)
    new_ref[...] = jnp.where(row16 == 14, fown_ref[12:13, :], new)
    again = [
        send(new_ref, nbr_ref.at[k], send2_sem.at[k], recv2_sem.at[k], there(d, -1))
        for k, d in enumerate(OFFSETS)
    ]
    for copy in again:
        copy.start()
    x2_ref[...] = x
    v2_ref[...] = v
    for copy in copies:
        copy.wait_send()
    for copy in again:
        copy.wait()


def last_kernel(
    fout_ref, fown_ref, x_ref, v_ref, rank_ref, xo_ref, vo_ref, fo_ref,
    back, stage, onehot, send_sem, recv_sem,
):
    greet([there(d, -1) for d in OFFSETS])
    copies = [
        send(fout_ref.at[k], back.at[k], send_sem.at[k], recv_sem.at[k], there(d, 1))
        for k, d in enumerate(OFFSETS)
    ]
    for copy in copies:
        copy.start()
    rank = rank_ref[...]
    for t in range(4):
        onehot[TILE * t : TILE * t + TILE, :] = chosen(rank, t)
    for copy in copies:
        copy.wait()
    total = fown_ref[...]
    for k in range(NBR):
        total = total + back[k]
    stage[0:16, :] = x_ref[...]
    stage[12:28, :] = v_ref[...] + HALF_STEP * total
    stage[24:40, :] = total
    stage[36:64, :] = jnp.zeros((28, TILE), F32)
    fields = jnp.concatenate([stage[pl.ds(t, 16, stride=4), :] for t in range(4)], 1)
    out = jnp.dot(split3(fields), onehot[...], preferred_element_type=F32)
    out = (out[32:48] + out[16:32]) + out[0:16]
    for f in range(3):
        xo_ref[f, 0, 0] = out[f : f + 1]
        vo_ref[f, 0, 0] = out[3 + f : 4 + f]
        fo_ref[f, 0, 0] = out[6 + f : 7 + f]


def place_kernel(*refs):
    copies = [pltpu.make_async_copy(refs[i], refs[3 + i], refs[6].at[i]) for i in range(3)]
    for copy in copies:
        copy.start()
    for copy in copies:
        copy.wait()


def call(kernel, outs, scratch, collective=None, ins=None, raw_in=False, raw_out=False, limit=24 << 20):
    vmem = pl.BlockSpec(memory_space=pltpu.VMEM)
    hbm = pl.BlockSpec(memory_space=pltpu.HBM)
    params = {"vmem_limit_bytes": limit}
    if collective is not None:
        params.update(collective_id=collective, has_side_effects=True)
    return pl.pallas_call(
        kernel,
        out_shape=tuple(jax.ShapeDtypeStruct(shape, kind) for shape, kind in outs),
        in_specs=[hbm if raw_in else vmem] * ins,
        out_specs=tuple(hbm if raw_out else vmem for _ in outs),
        scratch_shapes=scratch,
        compiler_params=pltpu.CompilerParams(**params),
    )


def on_device(
    positions, velocities, forces, charges, atom_types, tile_counts, pair_epsilon, pair_sigma
):
    dma = pltpu.SemaphoreType.DMA((NBR,))
    rows = ((16, TILE), F32)
    wide = (positions, velocities, forces, charges, atom_types)
    small = (tile_counts, pair_epsilon, pair_sigma)
    x, v, rec, rank = call(
        sort_kernel,
        (rows, rows, ((2, 16, TILE), F32), ((4, TILE), jnp.int32)),
        [pltpu.VMEM(given.shape, given.dtype) for given in wide]
        + [pltpu.SMEM(given.shape, given.dtype) for given in small]
        + [pltpu.VMEM((64, TILE), F32), pltpu.VMEM((64, TILE), F32), pltpu.SemaphoreType.DMA((8,))],
        ins=8,
        raw_in=True,
        limit=67043328,
    )(
        *wide, *small
    )
    (first,) = call(
        spread_kernel, (((NBR, 2, 16, TILE), F32),), [dma, dma], collective=0, ins=1
    )(rec)
    fout, fown = pair_forces(first, first, rec, rec, True)
    second, own, x, v = call(
        turn_kernel,
        (((NBR, 16, TILE), F32), rows, rows, rows),
        [pltpu.VMEM((NBR, 16, TILE), F32), dma, dma, dma, dma],
        collective=1,
        ins=5,
    )(fout, fown, x, v, rec)
    fout, fown = pair_forces(second, first, own, rec, False)
    flat = ((3, 1, 1, 1, 4 * TILE), F32)
    outs = call(
        last_kernel,
        (flat, flat, flat),
        [pltpu.VMEM((NBR, 16, TILE), F32), pltpu.VMEM((64, TILE), F32),
         pltpu.VMEM((512, 512), BF16), dma, dma],
        collective=2,
        ins=5,
    )(fout, fown, x, v, rank)
    return call(
        place_kernel, (flat, flat, flat), [pltpu.SemaphoreType.DMA((3,))], ins=3, raw_out=True
    )(*outs)


def solution(mesh):
    atoms = P(None, "gx", "gy", "gz", None)
    in_specs = (
        atoms, atoms, atoms,
        P("gx", "gy", "gz", None),
        P("gx", "gy", "gz", None),
        P("gx", "gy", "gz"),
        P(), P(),
    )
    return jax.shard_map(
        on_device, mesh=mesh, in_specs=in_specs, out_specs=(atoms,) * 3, check_vma=False
    )
```

```python
import functools

import jax
import jax.numpy as jnp
from jax import lax
from jax.experimental import pallas as pl
from jax.experimental.pallas import tpu as pltpu
from jax.sharding import PartitionSpec as P

TILE = 128
STEPS = 2
TIME_STEP = 0.05
HALF_STEP = 0.025
PLATE = ((1, 0), (1, 1), (0, 1), (-1, 1), (-1, 0), (-1, -1), (0, -1), (1, -1))
NP = len(PLATE)
OFFSETS = tuple((x, y, 0) for x, y in PLATE) + ((0, 0, -1), (0, 0, 1))
NBR = NP + 2
AXES = ("gx", "gy", "gz")
MESH = pl.DeviceIdType.MESH
F32 = jnp.float32
BF16 = jnp.bfloat16
FAR = 1e6
RIGHTS = 4 * (NP + 2)
RROWS = RIGHTS + 8
UNROLL = 8
PAD = 12
LOG2E = 1.4426950408889634
FORCE = 8.0 / (3.24 * 3.24)


def shares(first, pos_ref, par_ref, own_ref):
    row = lax.broadcasted_iota(jnp.int32, (64, TILE), 0)
    col = lax.broadcasted_iota(jnp.int32, (64, TILE), 1)
    lane = lax.broadcasted_iota(jnp.int32, (1, TILE), 1) >> 2
    lt, lbox, rt, rbox = row >> 4, (row >> 2) & 3, col & 3, col >> 2
    own_n = par_ref[NBR, 1, 12:13, :]
    nr = own_n
    for j in range(NP):
        nr = jnp.where(lane == j, par_ref[j, 1, 12:13, :], nr)
    below_n, above_n = par_ref[NP, 1, 12:13, :], par_ref[NP + 1, 1, 12:13, :]
    nl = jnp.where(lbox == 0, below_n, jnp.where(lbox == 2, above_n, own_n))
    nr = jnp.broadcast_to(nr, (64, TILE))
    ahead = (rbox < NP // 2) | ((rbox == NP) & (lbox == 2))
    left_first = (rbox < NP // 2) | ((rbox == NP) & (lbox == 0))
    lf, rf = lt.astype(F32), rt.astype(F32)
    order = jnp.where(left_first, lf * nr + rf, rf * nl + lf)
    if first:
        w1 = jnp.where(left_first, nl, nr)
        w2 = jnp.where(left_first, nr, nl)
    else:
        mine = own_ref[14:15, :]
        below, same, above = mine, mine, mine
        for j in range(NP):
            hit = lane == j
            below = jnp.where(hit, pos_ref[j, 12:13, :], below)
            same = jnp.where(hit, pos_ref[j, 14:15, :], same)
            above = jnp.where(hit, pos_ref[j, 13:14, :], above)
        below = jnp.where(lane == NP, pos_ref[NP, 14:15, :], below)
        above = jnp.where(lane == NP, pos_ref[NP + 1, 14:15, :], above)
        other = jnp.where(lbox == 0, below, jnp.where(lbox == 2, above, same))
        mine = jnp.broadcast_to(mine, (64, TILE))
        w1 = jnp.where(ahead, mine, other)
        w2 = jnp.where(ahead, other, mine)
    w1, w2 = w1 * w1 * w1, w2 * w2 * w2
    inside = (order + 0.5) * (w1 + w2) < w2 * (nl * nr)
    takes = jnp.where(inside, 1.0, 0.0)
    takes = jnp.where(ahead, takes, 1.0 - takes)
    shared = ((rbox < NP) & (lbox < 3)) | ((rbox == NP) & ((lbox == 0) | (lbox == 2)))
    alone = ((rbox == NP) & (lbox == 1) & (lt < rt)) | ((rbox == NP + 1) & (lbox == 1) & (lt == rt))
    return jnp.where(shared, takes, jnp.where(alone, 1.0, -1.0))


def pair_kernel(
    joined, pos_ref, par_ref, own_ref, fout_ref, fown_ref,
    left, right, acc_left, acc_right, list_v, list_s, sem,
):
    position = (lambda k: pos_ref[k, 0]) if joined else (lambda k: pos_ref[k])
    own = own_ref[NBR, 0] if joined else own_ref[...]
    row16 = lax.broadcasted_iota(jnp.int32, (16, 1), 0)
    lane16 = lax.broadcasted_iota(jnp.int32, (1, 16), 1)
    for k in range(NP + 2):
        if k < NP:
            p = position(k) + jnp.where(
                row16 < 4, float(PLATE[k][0]), jnp.where(row16 < 8, float(PLATE[k][1]), 0.0)
            )
            a = par_ref[k, 1]
        else:
            p, a = own, par_ref[NBR, 1]
        p = p * 2.0
        for f in range(3):
            right[f, 4 * k : 4 * k + 4, :] = p[4 * f : 4 * f + 4]
            right[3 + f, 4 * k : 4 * k + 4, :] = a[4 * f : 4 * f + 4]
    for f in range(6):
        right[f, RIGHTS:RROWS, :] = jnp.full((8, TILE), FAR if f < 3 else 0.0, F32)
    mins, maxs, downs = [], [], []
    scale = jnp.where(lane16 < 4, 0.04 / 6.0 * FORCE, jnp.where(lane16 < 8, 4.0 * FORCE, 1.0))
    for box in range(3):
        if box == 1:
            p, a = own, par_ref[NBR, 1]
        else:
            slot = NP if box == 0 else NP + 1
            p = position(slot) + jnp.where(
                (row16 >= 8) & (row16 < 12), -1.0 if box == 0 else 1.0, 0.0
            )
            a = par_ref[slot, 1]
        down = jnp.transpose(jnp.concatenate([p * 2.0, a], 0), (1, 0))
        blocks = down[:, :16].reshape(4, 32, 16)
        mins.append(jnp.min(blocks, axis=1))
        maxs.append(jnp.max(blocks, axis=1))
        downs.append(down)
    far = jnp.full((4, 16), FAR, F32)
    low = jnp.concatenate(mins + [far], 0)
    high = jnp.concatenate(maxs + [far], 0)
    gaps = jnp.zeros((64, TILE), F32)
    alive = None
    for f in range(3):
        a0 = jnp.concatenate([low[:, 4 * f + t : 4 * f + t + 1] for t in range(4)], 0)
        a1 = jnp.concatenate([high[:, 4 * f + t : 4 * f + t + 1] for t in range(4)], 0)
        v = jnp.concatenate([right[f], jnp.full((TILE - RROWS, TILE), FAR, F32)], 0)
        b0 = jnp.broadcast_to(jnp.min(v, axis=1, keepdims=True), (TILE, TILE))
        b1 = jnp.broadcast_to(jnp.max(v, axis=1, keepdims=True), (TILE, TILE))
        b0 = jnp.transpose(b0, (1, 0))[:1]
        b1 = jnp.transpose(b1, (1, 0))[:1]
        gap = jnp.maximum(jnp.maximum(a0 - b1, b0 - a1), 0.0)
        gaps = gaps + gap * gap
        if f == 0:
            alive = a0 < 0.1 * FAR
    mine = shares(joined, pos_ref, par_ref, own_ref)
    close = (gaps < 3.2401) & alive
    near = close & (mine > 0.5)
    weight = jnp.sum(jnp.where(close & (mine > -0.5), 1.0, 0.0), axis=0, keepdims=True)
    weight = jnp.sum(weight, axis=1, keepdims=True) + 1.0
    row = lax.broadcasted_iota(jnp.int32, (64, TILE), 0)
    r64 = lax.broadcasted_iota(jnp.int32, (64, 64), 0)
    c64 = lax.broadcasted_iota(jnp.int32, (64, 64), 1)
    ones = near.astype(F32)
    before = jnp.dot(
        (c64 < r64).astype(F32).astype(BF16), ones.astype(BF16), preferred_element_type=F32
    )
    place = jnp.where(near, before.astype(jnp.int32), -1)
    lane = lax.broadcasted_iota(jnp.int32, (1, TILE), 1)
    count = jnp.maximum(jnp.sum(ones, axis=0, keepdims=True), 1.0)
    total = jnp.sum(jnp.where(lane < RIGHTS, count, 0.0), axis=1, keepdims=True)
    count = jnp.where(lane < RIGHTS, count, 1e6).astype(jnp.int32)
    value = row - PAD
    for w in range(12):
        word = jnp.zeros((1, TILE), jnp.int32)
        for j in range(4):
            hit = jnp.where(place == 4 * w + j, value, 0)
            word = word + (jnp.sum(hit, axis=0, keepdims=True) + PAD) * (64**j)
        list_v[w : w + 1, :] = word
    list_v[12:13, :] = count
    list_v[13:14, :] = jnp.broadcast_to(total, (1, TILE)).astype(jnp.int32)
    copy = pltpu.make_async_copy(list_v, list_s, sem)
    copy.start()
    for box, down in enumerate(downs):
        scaled = down[:, 16:] * scale
        for t in range(4):
            base = (t * 16 + box * 4) * 4
            for f in range(6):
                at = 4 * (f % 3) + t
                source = down if f < 3 else scaled
                left[f, base : base + 16] = jnp.broadcast_to(
                    source[:, at : at + 1], (TILE, TILE)
                ).reshape(16, 8, TILE)
    for f in range(6):
        left[f, 4 * PAD : 4 * PAD + 4] = jnp.full((4, 8, TILE), FAR if f < 3 else 0.0, F32)
    acc_left[...] = jnp.zeros_like(acc_left)
    acc_right[...] = jnp.zeros_like(acc_right)
    copy.wait()

    def turn(_, state):
        r, k = state
        for _ in range(UNROLL):
            b = ((list_s[k >> 2, r] >> ((k & 3) * 6)) & 63) * 4
            at = pl.ds(b, 4)
            rx, ry, rz, rq, re, rs_ = [
                jnp.broadcast_to(right[f, pl.ds(r, 1), :], (8, TILE))[None] for f in range(6)
            ]
            dx = left[0, at] - rx
            dy = left[1, at] - ry
            dz = left[2, at] - rz
            s2 = (dx * dx + 0.09) + dy * dy + dz * dz
            rs = lax.rsqrt(s2)
            inv = rs * rs
            screen = jnp.exp2(s2 * (-LOG2E) * rs)
            w = jnp.maximum(3.33 - s2, 0.0)
            slope = (w * inv) * 1.5
            one = slope + 1.0
            two = one + slope
            size = left[5, at] + rs_
            ratio = size * size * inv
            cubed = ratio * ratio * ratio
            lennard = (left[4, at] * re) * cubed * (cubed * two - one)
            coulomb = (left[3, at] * rq) * screen * (rs * (one + 5.0) + slope)
            g = (lennard + coulomb) * w
            fx, fy, fz = g * dx, g * dy, g * dz
            acc_left[0, at] += fx
            acc_left[1, at] += fy
            acc_left[2, at] += fz
            acc_right[0, r] -= jnp.sum(fx, axis=0)
            acc_right[1, r] -= jnp.sum(fy, axis=0)
            acc_right[2, r] -= jnp.sum(fz, axis=0)
            on = k + 1 >= list_s[12, r]
            k = jnp.where(on, 0, k + 1)
            r = jnp.where(on, r + 1, r)
        return r, k

    lax.fori_loop(0, (list_s[13, 0] + UNROLL - 1) // UNROLL, turn, (jnp.int32(0), jnp.int32(0)))
    tail = jnp.broadcast_to(weight, (4, TILE))

    def gathered(k):
        rows = [jnp.sum(acc_right[f, 4 * k : 4 * k + 4], axis=1) for f in range(3)]
        return jnp.concatenate(rows + [tail], 0)

    for k in range(NP):
        fout_ref[k] = gathered(k)
    ones = [
        jnp.where(lax.broadcasted_iota(jnp.int32, (2 * TILE, TILE), 1) == f, 1.0, 0.0).astype(BF16)
        for f in range(3)
    ]
    ones = jnp.concatenate(ones, 0)
    for box in range(3):
        parts = []
        for t in range(4):
            base = (t * 16 + box * 4) * 4
            halves = []
            for f in range(3):
                a = acc_left[f, base : base + 16].reshape(TILE, TILE)
                hi = a.astype(BF16)
                halves += [hi, (a - hi.astype(F32)).astype(BF16)]
            parts.append(jnp.concatenate(halves, 1))
        sums = jnp.dot(jnp.concatenate(parts, 0), ones, preferred_element_type=F32)
        target = fown_ref if box == 1 else fout_ref.at[NP if box == 0 else NP + 1]
        other = gathered(NP)
        for t in range(4):
            row = jnp.transpose(sums[TILE * t : TILE * t + TILE], (1, 0))
            for f in range(3):
                at = 4 * f + t
                value = row[f : f + 1]
                target[at : at + 1, :] = value + other[at : at + 1] if box == 1 else value
        target[12:16, :] = tail


def pair_forces(pos, par, own, joined):
    vmem = pl.BlockSpec(memory_space=pltpu.VMEM)
    return pl.pallas_call(
        functools.partial(pair_kernel, joined),
        out_shape=(
            jax.ShapeDtypeStruct((NBR, 16, TILE), F32),
            jax.ShapeDtypeStruct((16, TILE), F32),
        ),
        in_specs=[vmem] * 3,
        out_specs=(vmem, vmem),
        scratch_shapes=[
            pltpu.VMEM((6, 256, 8, TILE), F32),
            pltpu.VMEM((6, RROWS, TILE), F32),
            pltpu.VMEM((3, 256, 8, TILE), F32),
            pltpu.VMEM((3, RROWS, 8, TILE), F32),
            pltpu.VMEM((16, TILE), jnp.int32),
            pltpu.SMEM((16, TILE), jnp.int32),
            pltpu.SemaphoreType.DMA,
        ],
        compiler_params=pltpu.CompilerParams(vmem_limit_bytes=24 << 20),
    )(pos, par, own)


def hilbert(cells, bits):
    x = list(cells)
    q = 1 << (bits - 1)
    while q > 1:
        p = q - 1
        for i in range(3):
            hit = (x[i] & q) != 0
            if i == 0:
                x[0] = jnp.where(hit, x[0] ^ p, x[0])
            else:
                swap = (x[0] ^ x[i]) & p
                x[0], x[i] = jnp.where(hit, x[0] ^ p, x[0] ^ swap), jnp.where(hit, x[i], x[i] ^ swap)
        q >>= 1
    x[1] = x[1] ^ x[0]
    x[2] = x[2] ^ x[1]
    flip = jnp.zeros_like(x[0])
    q = 1 << (bits - 1)
    while q > 1:
        flip = jnp.where((x[2] & q) != 0, flip ^ (q - 1), flip)
        q >>= 1
    x = [v ^ flip for v in x]
    key = jnp.zeros_like(x[0])
    for bit in range(bits - 1, -1, -1):
        for a in range(3):
            key = key * 2 + ((x[a] >> bit) & 1)
    return key


def split3(a):
    hi = a.astype(BF16)
    rest = a - hi.astype(F32)
    mid = rest.astype(BF16)
    lo = (rest - mid.astype(F32)).astype(BF16)
    return jnp.concatenate([hi, mid, lo], 0)


def chosen(rank, t):
    place = lax.broadcasted_iota(jnp.int32, (TILE, TILE), 0) + TILE * t
    tiles = [(rank[j : j + 1, :] == place).astype(F32).astype(BF16) for j in range(4)]
    return jnp.concatenate(tiles, 1)


def there(offset, sign):
    return tuple(
        lax.rem(lax.axis_index(a) + sign * o + lax.axis_size(a), lax.axis_size(a))
        for a, o in zip(AXES, offset)
    )


def hail(offsets):
    barrier = pltpu.get_barrier_semaphore()
    for d in offsets:
        pl.semaphore_signal(barrier, inc=1, device_id=there(d, 1), device_id_type=MESH)


def meet(offsets):
    pl.semaphore_wait(pltpu.get_barrier_semaphore(), len(offsets))


def send(source, target, send_sem, recv_sem, device):
    return pltpu.make_async_remote_copy(
        src_ref=source,
        dst_ref=target,
        send_sem=send_sem,
        recv_sem=recv_sem,
        device_id=device,
        device_id_type=MESH,
    )


def first_kernel(*refs):
    given, (x_ref, v_ref, all_ref, rank_ref), held = refs[:8], refs[8:12], refs[12:20]
    stage, staged, rec, sem, send_sem, recv_sem = refs[20:]
    hail(OFFSETS)
    copies = [
        pltpu.make_async_copy(source, target, sem.at[i])
        for i, (source, target) in enumerate(zip(given, held))
    ]
    for copy in copies:
        copy.start()
    for copy in copies:
        copy.wait()
    pos_ref, vel_ref, frc_ref, chg_ref, typ_ref, count_ref, eps_ref, sig_ref = held

    def rows(ref, f):
        return [ref[f, 0, 0, :, TILE * t : TILE * t + TILE] for t in range(4)]

    def rows1(ref):
        return [ref[0, 0, :, TILE * t : TILE * t + TILE] for t in range(4)]

    def flat(ref):
        return jnp.concatenate([row for f in range(3) for row in rows(ref, f)], 0)

    v = flat(vel_ref) + HALF_STEP * flat(frc_ref)
    x = flat(pos_ref) + TIME_STEP * v
    count = count_ref[0, 0, 0]
    row = lax.broadcasted_iota(jnp.int32, (4, TILE), 0)
    live = row < count
    kinds = jnp.concatenate(rows1(typ_ref), 0)
    eps = jnp.zeros((4, TILE), F32)
    sig = jnp.zeros((4, TILE), F32)
    for k in range(eps_ref.shape[0]):
        eps = jnp.where(kinds == k, eps_ref[k], eps)
        sig = jnp.where(kinds == k, sig_ref[k], sig)
    alive = live.astype(F32)
    stage[...] = jnp.zeros_like(stage)
    stage[0:12, :] = x
    stage[12:24, :] = v
    stage[24:28, :] = jnp.concatenate(rows1(chg_ref), 0) * alive
    stage[28:32, :] = jnp.sqrt(eps) * alive
    stage[32:36, :] = sig
    cells = [
        jnp.clip((jnp.clip(x[4 * a : 4 * a + 4], -1.0, 2.0) * 4.0).astype(jnp.int32), 0, 3)
        for a in range(3)
    ]
    index = row * TILE + lax.broadcasted_iota(jnp.int32, (4, TILE), 1)
    key = jnp.where(live, hilbert(cells, 2), 64) * 512 + index
    key = jnp.concatenate([key.astype(F32), jnp.zeros((4, TILE), F32)], 0)
    down = jnp.transpose(key, (1, 0))
    ranks = []
    for j in range(4):
        less = jnp.zeros((TILE, TILE), F32)
        for i in range(4):
            less = less + (down[:, i : i + 1] < key[j : j + 1, :]).astype(F32)
        ranks.append(jnp.sum(less, axis=0, keepdims=True))
    rank = jnp.concatenate(ranks, 0).astype(jnp.int32)
    rank_ref[...] = rank
    fields = jnp.concatenate([stage[pl.ds(t, 16, stride=4), :] for t in range(4)], 1)
    parts = split3(fields)
    for t in range(4):
        out = lax.dot_general(
            parts, chosen(rank, t), (((1,), (1,)), ((), ())), preferred_element_type=F32
        )
        staged[pl.ds(t, 16, stride=4), :] = (out[32:48] + out[16:32]) + out[0:16]
    row16 = lax.broadcasted_iota(jnp.int32, (16, TILE), 0)
    place = staged[0:16, :]
    x_ref[...] = place
    v_ref[...] = staged[12:28, :]
    rec[0] = jnp.where((row16 & 3) < count, place, FAR)
    rec[1] = jnp.where(row16 < 12, staged[24:40, :], count.astype(F32))
    meet(OFFSETS)
    copies = [
        send(rec, all_ref.at[k], send_sem.at[k], recv_sem.at[k], there(d, -1))
        for k, d in enumerate(OFFSETS)
    ]
    for copy in copies:
        copy.start()
    own = pltpu.make_async_copy(rec, all_ref.at[NBR], sem.at[8])
    own.start()
    own.wait()
    for copy in copies:
        copy.wait()


def turn_kernel(
    fout_ref, fown_ref, x_ref, v_ref, old_ref,
    nbr_ref, new_ref, x2_ref, v2_ref,
    back, send_sem, recv_sem, send2_sem, recv2_sem,
):
    hail(OFFSETS)
    meet(OFFSETS)
    copies = [
        send(fout_ref.at[k], back.at[k], send_sem.at[k], recv_sem.at[k], there(d, 1))
        for k, d in enumerate(OFFSETS)
    ]
    for copy in copies:
        copy.start()
    for copy in copies:
        copy.wait_recv()
    total = fown_ref[...]
    for k in range(NBR):
        total = total + back[k]
    v = v_ref[...] + HALF_STEP * total
    v = v + HALF_STEP * total
    x = x_ref[...] + TIME_STEP * v
    row16 = lax.broadcasted_iota(jnp.int32, (16, TILE), 0)
    new = jnp.where(old_ref[NBR, 0] > 0.1 * FAR, FAR, x)
    new = jnp.where(row16 == 12, back[NP + 1, 12:13, :], new)
    new = jnp.where(row16 == 13, back[NP, 12:13, :], new)
    new_ref[...] = jnp.where(row16 == 14, fown_ref[12:13, :], new)
    again = [
        send(new_ref, nbr_ref.at[k], send2_sem.at[k], recv2_sem.at[k], there(d, -1))
        for k, d in enumerate(OFFSETS)
    ]
    for copy in again:
        copy.start()
    x2_ref[...] = x
    v2_ref[...] = v
    for copy in copies:
        copy.wait_send()
    for copy in again:
        copy.wait()


def last_kernel(
    fout_ref, fown_ref, x_ref, v_ref, rank_ref, xo_ref, vo_ref, fo_ref,
    back, stage, onehot, send_sem, recv_sem,
):
    hail(OFFSETS)
    meet(OFFSETS)
    copies = [
        send(fout_ref.at[k], back.at[k], send_sem.at[k], recv_sem.at[k], there(d, 1))
        for k, d in enumerate(OFFSETS)
    ]
    for copy in copies:
        copy.start()
    rank = rank_ref[...]
    for t in range(4):
        onehot[TILE * t : TILE * t + TILE, :] = chosen(rank, t)
    for copy in copies:
        copy.wait()
    total = fown_ref[...]
    for k in range(NBR):
        total = total + back[k]
    stage[0:16, :] = x_ref[...]
    stage[12:28, :] = v_ref[...] + HALF_STEP * total
    stage[24:40, :] = total
    stage[36:64, :] = jnp.zeros((28, TILE), F32)
    fields = jnp.concatenate([stage[pl.ds(t, 16, stride=4), :] for t in range(4)], 1)
    out = jnp.dot(split3(fields), onehot[...], preferred_element_type=F32)
    out = (out[32:48] + out[16:32]) + out[0:16]
    for f in range(3):
        xo_ref[f, 0, 0] = out[f : f + 1]
        vo_ref[f, 0, 0] = out[3 + f : 4 + f]
        fo_ref[f, 0, 0] = out[6 + f : 7 + f]


def place_kernel(*refs):
    copies = [pltpu.make_async_copy(refs[i], refs[3 + i], refs[6].at[i]) for i in range(3)]
    for copy in copies:
        copy.start()
    for copy in copies:
        copy.wait()


def call(kernel, outs, scratch, collective=None, ins=None, raw_in=False, raw_out=False, limit=24 << 20):
    vmem = pl.BlockSpec(memory_space=pltpu.VMEM)
    hbm = pl.BlockSpec(memory_space=pltpu.HBM)
    params = {"vmem_limit_bytes": limit}
    if collective is not None:
        params.update(collective_id=collective, has_side_effects=True)
    return pl.pallas_call(
        kernel,
        out_shape=tuple(jax.ShapeDtypeStruct(shape, kind) for shape, kind in outs),
        in_specs=[hbm if raw_in else vmem] * ins,
        out_specs=tuple(hbm if raw_out else vmem for _ in outs),
        scratch_shapes=scratch,
        compiler_params=pltpu.CompilerParams(**params),
    )


def on_device(
    positions, velocities, forces, charges, atom_types, tile_counts, pair_epsilon, pair_sigma
):
    dma = pltpu.SemaphoreType.DMA((NBR,))
    rows = ((16, TILE), F32)
    wide = (positions, velocities, forces, charges, atom_types)
    small = (tile_counts, pair_epsilon, pair_sigma)
    x, v, first, rank = call(
        first_kernel,
        (rows, rows, ((NBR + 1, 2, 16, TILE), F32), ((4, TILE), jnp.int32)),
        [pltpu.VMEM(given.shape, given.dtype) for given in wide]
        + [pltpu.SMEM(given.shape, given.dtype) for given in small]
        + [pltpu.VMEM((64, TILE), F32), pltpu.VMEM((64, TILE), F32), pltpu.VMEM((2, 16, TILE), F32),
           pltpu.SemaphoreType.DMA((9,)), dma, dma],
        collective=0,
        ins=8,
        raw_in=True,
        limit=67043328,
    )(
        *wide, *small
    )
    fout, fown = pair_forces(first, first, first, True)
    second, own, x, v = call(
        turn_kernel,
        (((NBR, 16, TILE), F32), rows, rows, rows),
        [pltpu.VMEM((NBR, 16, TILE), F32), dma, dma, dma, dma],
        collective=1,
        ins=5,
    )(fout, fown, x, v, first)
    fout, fown = pair_forces(second, first, own, False)
    flat = ((3, 1, 1, 1, 4 * TILE), F32)
    outs = call(
        last_kernel,
        (flat, flat, flat),
        [pltpu.VMEM((NBR, 16, TILE), F32), pltpu.VMEM((64, TILE), F32),
         pltpu.VMEM((512, 512), BF16), dma, dma],
        collective=2,
        ins=5,
    )(fout, fown, x, v, rank)
    return call(
        place_kernel, (flat, flat, flat), [pltpu.SemaphoreType.DMA((3,))], ins=3, raw_out=True
    )(*outs)


def solution(mesh):
    atoms = P(None, "gx", "gy", "gz", None)
    in_specs = (
        atoms, atoms, atoms,
        P("gx", "gy", "gz", None),
        P("gx", "gy", "gz", None),
        P("gx", "gy", "gz"),
        P(), P(),
    )
    return jax.shard_map(
        on_device, mesh=mesh, in_specs=in_specs, out_specs=(atoms,) * 3, check_vma=False
    )
```

```python
import functools

import jax
import jax.numpy as jnp
from jax import lax
from jax.experimental import pallas as pl
from jax.experimental.pallas import tpu as pltpu
from jax.sharding import PartitionSpec as P

TILE = 128
STEPS = 2
TIME_STEP = 0.05
HALF_STEP = 0.025
PLATE = ((1, 0), (1, 1), (0, 1), (-1, 1), (-1, 0), (-1, -1), (0, -1), (1, -1))
NP = len(PLATE)
OFFSETS = tuple((x, y, 0) for x, y in PLATE) + ((0, 0, -1), (0, 0, 1))
NBR = NP + 2
AXES = ("gx", "gy", "gz")
MESH = pl.DeviceIdType.MESH
F32 = jnp.float32
BF16 = jnp.bfloat16
FAR = 1e6
RIGHTS = 4 * (NP + 2)
RROWS = RIGHTS + 8
UNROLL = 8
PAD = 12
LOG2E = 1.4426950408889634
FORCE = 8.0 / (3.24 * 3.24)


def shares(first, pos_ref, par_ref, own_ref):
    row = lax.broadcasted_iota(jnp.int32, (64, TILE), 0)
    col = lax.broadcasted_iota(jnp.int32, (64, TILE), 1)
    lane = lax.broadcasted_iota(jnp.int32, (1, TILE), 1) >> 2
    lt, lbox, rt, rbox = row >> 4, (row >> 2) & 3, col & 3, col >> 2
    own_n = par_ref[NBR, 1, 12:13, :]
    nr = own_n
    for j in range(NP):
        nr = jnp.where(lane == j, par_ref[j, 1, 12:13, :], nr)
    below_n, above_n = par_ref[NP, 1, 12:13, :], par_ref[NP + 1, 1, 12:13, :]
    nl = jnp.where(lbox == 0, below_n, jnp.where(lbox == 2, above_n, own_n))
    nr = jnp.broadcast_to(nr, (64, TILE))
    ahead = (rbox < NP // 2) | ((rbox == NP) & (lbox == 2))
    left_first = (rbox < NP // 2) | ((rbox == NP) & (lbox == 0))
    lf, rf = lt.astype(F32), rt.astype(F32)
    order = jnp.where(left_first, lf * nr + rf, rf * nl + lf)
    if first:
        w1 = jnp.where(left_first, nl, nr)
        w2 = jnp.where(left_first, nr, nl)
    else:
        mine = own_ref[14:15, :]
        below, same, above = mine, mine, mine
        for j in range(NP):
            hit = lane == j
            below = jnp.where(hit, pos_ref[j, 12:13, :], below)
            same = jnp.where(hit, pos_ref[j, 14:15, :], same)
            above = jnp.where(hit, pos_ref[j, 13:14, :], above)
        below = jnp.where(lane == NP, pos_ref[NP, 14:15, :], below)
        above = jnp.where(lane == NP, pos_ref[NP + 1, 14:15, :], above)
        other = jnp.where(lbox == 0, below, jnp.where(lbox == 2, above, same))
        mine = jnp.broadcast_to(mine, (64, TILE))
        w1 = jnp.where(ahead, mine, other)
        w2 = jnp.where(ahead, other, mine)
    w1, w2 = w1 * w1 * w1, w2 * w2 * w2
    inside = (order + 0.5) * (w1 + w2) < w2 * (nl * nr)
    takes = jnp.where(inside, 1.0, 0.0)
    takes = jnp.where(ahead, takes, 1.0 - takes)
    shared = ((rbox < NP) & (lbox < 3)) | ((rbox == NP) & ((lbox == 0) | (lbox == 2)))
    alone = ((rbox == NP) & (lbox == 1) & (lt < rt)) | ((rbox == NP + 1) & (lbox == 1) & (lt == rt))
    return jnp.where(shared, takes, jnp.where(alone, 1.0, -1.0))


def pair_kernel(
    joined, pos_ref, par_ref, own_ref, fout_ref, fown_ref,
    left, right, acc_left, acc_right, list_v, list_s, sem,
):
    position = (lambda k: pos_ref[k, 0]) if joined else (lambda k: pos_ref[k])
    own = own_ref[NBR, 0] if joined else own_ref[...]
    row16 = lax.broadcasted_iota(jnp.int32, (16, 1), 0)
    lane16 = lax.broadcasted_iota(jnp.int32, (1, 16), 1)
    for k in range(NP + 2):
        if k < NP:
            p = position(k) + jnp.where(
                row16 < 4, float(PLATE[k][0]), jnp.where(row16 < 8, float(PLATE[k][1]), 0.0)
            )
            a = par_ref[k, 1]
        else:
            p, a = own, par_ref[NBR, 1]
        p = p * 2.0
        for f in range(3):
            right[f, 4 * k : 4 * k + 4, :] = p[4 * f : 4 * f + 4]
            right[3 + f, 4 * k : 4 * k + 4, :] = a[4 * f : 4 * f + 4]
    for f in range(6):
        right[f, RIGHTS:RROWS, :] = jnp.full((8, TILE), FAR if f < 3 else 0.0, F32)
    mins, maxs, downs = [], [], []
    scale = jnp.where(lane16 < 4, 0.04 / 6.0 * FORCE, jnp.where(lane16 < 8, 4.0 * FORCE, 1.0))
    for box in range(3):
        if box == 1:
            p, a = own, par_ref[NBR, 1]
        else:
            slot = NP if box == 0 else NP + 1
            p = position(slot) + jnp.where(
                (row16 >= 8) & (row16 < 12), -1.0 if box == 0 else 1.0, 0.0
            )
            a = par_ref[slot, 1]
        down = jnp.transpose(jnp.concatenate([p * 2.0, a], 0), (1, 0))
        blocks = down[:, :16].reshape(4, 32, 16)
        mins.append(jnp.min(blocks, axis=1))
        maxs.append(jnp.max(blocks, axis=1))
        downs.append(down)
    far = jnp.full((4, 16), FAR, F32)
    low = jnp.concatenate(mins + [far], 0)
    high = jnp.concatenate(maxs + [far], 0)
    gaps = jnp.zeros((64, TILE), F32)
    alive = None
    for f in range(3):
        a0 = jnp.concatenate([low[:, 4 * f + t : 4 * f + t + 1] for t in range(4)], 0)
        a1 = jnp.concatenate([high[:, 4 * f + t : 4 * f + t + 1] for t in range(4)], 0)
        v = jnp.concatenate([right[f], jnp.full((TILE - RROWS, TILE), FAR, F32)], 0)
        b0 = jnp.broadcast_to(jnp.min(v, axis=1, keepdims=True), (TILE, TILE))
        b1 = jnp.broadcast_to(jnp.max(v, axis=1, keepdims=True), (TILE, TILE))
        b0 = jnp.transpose(b0, (1, 0))[:1]
        b1 = jnp.transpose(b1, (1, 0))[:1]
        gap = jnp.maximum(jnp.maximum(a0 - b1, b0 - a1), 0.0)
        gaps = gaps + gap * gap
        if f == 0:
            alive = a0 < 0.1 * FAR
    mine = shares(joined, pos_ref, par_ref, own_ref)
    close = (gaps < 3.2401) & alive
    near = close & (mine > 0.5)
    weight = jnp.sum(jnp.where(close & (mine > -0.5), 1.0, 0.0), axis=0, keepdims=True)
    weight = jnp.sum(weight, axis=1, keepdims=True) + 1.0
    row = lax.broadcasted_iota(jnp.int32, (64, TILE), 0)
    r64 = lax.broadcasted_iota(jnp.int32, (64, 64), 0)
    c64 = lax.broadcasted_iota(jnp.int32, (64, 64), 1)
    ones = near.astype(F32)
    before = jnp.dot(
        (c64 < r64).astype(F32).astype(BF16), ones.astype(BF16), preferred_element_type=F32
    )
    place = jnp.where(near, before.astype(jnp.int32), -1)
    lane = lax.broadcasted_iota(jnp.int32, (1, TILE), 1)
    count = jnp.maximum(jnp.sum(ones, axis=0, keepdims=True), 1.0)
    total = jnp.sum(jnp.where(lane < RIGHTS, count, 0.0), axis=1, keepdims=True)
    count = jnp.where(lane < RIGHTS, count, 1e6).astype(jnp.int32)
    value = row - PAD
    for w in range(12):
        word = jnp.zeros((1, TILE), jnp.int32)
        for j in range(4):
            hit = jnp.where(place == 4 * w + j, value, 0)
            word = word + (jnp.sum(hit, axis=0, keepdims=True) + PAD) * (64**j)
        list_v[w : w + 1, :] = word
    list_v[12:13, :] = count
    list_v[13:14, :] = jnp.broadcast_to(total, (1, TILE)).astype(jnp.int32)
    copy = pltpu.make_async_copy(list_v, list_s, sem)
    copy.start()
    wanted = (lax.broadcasted_iota(jnp.int32, (48, 4 * TILE), 0) & 15) - (
        lax.broadcasted_iota(jnp.int32, (48, 4 * TILE), 1) >> 7
    )
    picks = [jnp.where(wanted == 4 * f, 1.0, 0.0).astype(BF16) for f in range(3)]
    for box, down in enumerate(downs):
        scaled = down[:, 16:] * scale
        for f in range(0, 6):
            source = down[:, :16] if f < 3 else scaled
            hi = source.astype(BF16)
            rest = source - hi.astype(F32)
            mid = rest.astype(BF16)
            pieces = jnp.concatenate([hi, mid, (rest - mid.astype(F32)).astype(BF16)], 1)
            wide = jnp.dot(pieces, picks[f % 3], preferred_element_type=F32)
            for t in range(4):
                base = (t * 16 + box * 4) * 4
                left[f, base : base + 16] = wide[:, TILE * t : TILE * t + TILE].reshape(16, 8, TILE)
    for f in range(6):
        left[f, 4 * PAD : 4 * PAD + 4] = jnp.full((4, 8, TILE), FAR if f < 3 else 0.0, F32)
    acc_left[...] = jnp.zeros_like(acc_left)
    acc_right[...] = jnp.zeros_like(acc_right)
    copy.wait()

    def turn(_, state):
        r, k = state
        for _ in range(UNROLL):
            b = ((list_s[k >> 2, r] >> ((k & 3) * 6)) & 63) * 4
            at = pl.ds(b, 4)
            rx, ry, rz, rq, re, rs_ = [
                jnp.broadcast_to(right[f, pl.ds(r, 1), :], (8, TILE))[None] for f in range(6)
            ]
            dx = left[0, at] - rx
            dy = left[1, at] - ry
            dz = left[2, at] - rz
            s2 = (dx * dx + 0.09) + dy * dy + dz * dz
            rs = lax.rsqrt(s2)
            inv = rs * rs
            screen = jnp.exp2(s2 * (-LOG2E) * rs)
            w = jnp.maximum(3.33 - s2, 0.0)
            slope = (w * inv) * 1.5
            one = slope + 1.0
            two = one + slope
            size = left[5, at] + rs_
            ratio = size * size * inv
            cubed = ratio * ratio * ratio
            lennard = (left[4, at] * re) * cubed * (cubed * two - one)
            coulomb = (left[3, at] * rq) * screen * (rs * (one + 5.0) + slope)
            g = (lennard + coulomb) * w
            fx, fy, fz = g * dx, g * dy, g * dz
            acc_left[0, at] += fx
            acc_left[1, at] += fy
            acc_left[2, at] += fz
            acc_right[0, r] -= jnp.sum(fx, axis=0)
            acc_right[1, r] -= jnp.sum(fy, axis=0)
            acc_right[2, r] -= jnp.sum(fz, axis=0)
            on = k + 1 >= list_s[12, r]
            k = jnp.where(on, 0, k + 1)
            r = jnp.where(on, r + 1, r)
        return r, k

    lax.fori_loop(0, (list_s[13, 0] + UNROLL - 1) // UNROLL, turn, (jnp.int32(0), jnp.int32(0)))
    tail = jnp.broadcast_to(weight, (4, TILE))

    def gathered(k):
        rows = [jnp.sum(acc_right[f, 4 * k : 4 * k + 4], axis=1) for f in range(3)]
        return jnp.concatenate(rows + [tail], 0)

    for k in range(NP):
        fout_ref[k] = gathered(k)
    ones = [
        jnp.where(lax.broadcasted_iota(jnp.int32, (2 * TILE, TILE), 1) == f, 1.0, 0.0).astype(BF16)
        for f in range(3)
    ]
    ones = jnp.concatenate(ones, 0)
    for box in range(3):
        parts = []
        for t in range(4):
            base = (t * 16 + box * 4) * 4
            halves = []
            for f in range(3):
                a = acc_left[f, base : base + 16].reshape(TILE, TILE)
                hi = a.astype(BF16)
                halves += [hi, (a - hi.astype(F32)).astype(BF16)]
            parts.append(jnp.concatenate(halves, 1))
        sums = jnp.dot(jnp.concatenate(parts, 0), ones, preferred_element_type=F32)
        target = fown_ref if box == 1 else fout_ref.at[NP if box == 0 else NP + 1]
        other = gathered(NP)
        for t in range(4):
            row = jnp.transpose(sums[TILE * t : TILE * t + TILE], (1, 0))
            for f in range(3):
                at = 4 * f + t
                value = row[f : f + 1]
                target[at : at + 1, :] = value + other[at : at + 1] if box == 1 else value
        target[12:16, :] = tail


def pair_forces(pos, par, own, joined):
    vmem = pl.BlockSpec(memory_space=pltpu.VMEM)
    return pl.pallas_call(
        functools.partial(pair_kernel, joined),
        out_shape=(
            jax.ShapeDtypeStruct((NBR, 16, TILE), F32),
            jax.ShapeDtypeStruct((16, TILE), F32),
        ),
        in_specs=[vmem] * 3,
        out_specs=(vmem, vmem),
        scratch_shapes=[
            pltpu.VMEM((6, 256, 8, TILE), F32),
            pltpu.VMEM((6, RROWS, TILE), F32),
            pltpu.VMEM((3, 256, 8, TILE), F32),
            pltpu.VMEM((3, RROWS, 8, TILE), F32),
            pltpu.VMEM((16, TILE), jnp.int32),
            pltpu.SMEM((16, TILE), jnp.int32),
            pltpu.SemaphoreType.DMA,
        ],
        compiler_params=pltpu.CompilerParams(vmem_limit_bytes=24 << 20),
    )(pos, par, own)


def hilbert(cells, bits):
    x = list(cells)
    q = 1 << (bits - 1)
    while q > 1:
        p = q - 1
        for i in range(3):
            hit = (x[i] & q) != 0
            if i == 0:
                x[0] = jnp.where(hit, x[0] ^ p, x[0])
            else:
                swap = (x[0] ^ x[i]) & p
                x[0], x[i] = jnp.where(hit, x[0] ^ p, x[0] ^ swap), jnp.where(hit, x[i], x[i] ^ swap)
        q >>= 1
    x[1] = x[1] ^ x[0]
    x[2] = x[2] ^ x[1]
    flip = jnp.zeros_like(x[0])
    q = 1 << (bits - 1)
    while q > 1:
        flip = jnp.where((x[2] & q) != 0, flip ^ (q - 1), flip)
        q >>= 1
    x = [v ^ flip for v in x]
    key = jnp.zeros_like(x[0])
    for bit in range(bits - 1, -1, -1):
        for a in range(3):
            key = key * 2 + ((x[a] >> bit) & 1)
    return key


def split3(a):
    hi = a.astype(BF16)
    rest = a - hi.astype(F32)
    mid = rest.astype(BF16)
    lo = (rest - mid.astype(F32)).astype(BF16)
    return jnp.concatenate([hi, mid, lo], 0)


def chosen(rank, t):
    place = (lax.broadcasted_iota(jnp.int32, (TILE, TILE), 0) + TILE * t).astype(F32)
    tiles = [(rank[j : j + 1, :] == place).astype(F32).astype(BF16) for j in range(4)]
    return jnp.concatenate(tiles, 1)


def there(offset, sign):
    return tuple(
        lax.rem(lax.axis_index(a) + sign * o + lax.axis_size(a), lax.axis_size(a))
        for a, o in zip(AXES, offset)
    )


def hail(offsets):
    barrier = pltpu.get_barrier_semaphore()
    for d in offsets:
        pl.semaphore_signal(barrier, inc=1, device_id=there(d, 1), device_id_type=MESH)


def meet(offsets):
    pl.semaphore_wait(pltpu.get_barrier_semaphore(), len(offsets))


def send(source, target, send_sem, recv_sem, device):
    return pltpu.make_async_remote_copy(
        src_ref=source,
        dst_ref=target,
        send_sem=send_sem,
        recv_sem=recv_sem,
        device_id=device,
        device_id_type=MESH,
    )


def first_kernel(*refs):
    given, (x_ref, v_ref, all_ref), held = refs[:8], refs[8:11], refs[11:19]
    stage, staged, rec, sem, send_sem, recv_sem = refs[19:]
    hail(OFFSETS)
    copies = [
        pltpu.make_async_copy(source, target, sem.at[i])
        for i, (source, target) in enumerate(zip(given, held))
    ]
    for copy in copies:
        copy.start()
    for copy in copies:
        copy.wait()
    pos_ref, vel_ref, frc_ref, chg_ref, typ_ref, count_ref, eps_ref, sig_ref = held

    def rows(ref, f):
        return [ref[f, 0, 0, :, TILE * t : TILE * t + TILE] for t in range(4)]

    def rows1(ref):
        return [ref[0, 0, :, TILE * t : TILE * t + TILE] for t in range(4)]

    def flat(ref):
        return jnp.concatenate([row for f in range(3) for row in rows(ref, f)], 0)

    v = flat(vel_ref) + HALF_STEP * flat(frc_ref)
    x = flat(pos_ref) + TIME_STEP * v
    count = count_ref[0, 0, 0]
    row = lax.broadcasted_iota(jnp.int32, (4, TILE), 0)
    live = row < count
    kinds = jnp.concatenate(rows1(typ_ref), 0)
    eps = jnp.zeros((4, TILE), F32)
    sig = jnp.zeros((4, TILE), F32)
    for k in range(eps_ref.shape[0]):
        eps = jnp.where(kinds == k, eps_ref[k], eps)
        sig = jnp.where(kinds == k, sig_ref[k], sig)
    alive = live.astype(F32)
    stage[...] = jnp.zeros_like(stage)
    stage[0:12, :] = x
    stage[12:24, :] = v
    stage[24:28, :] = jnp.concatenate(rows1(chg_ref), 0) * alive
    stage[28:32, :] = jnp.sqrt(eps) * alive
    stage[32:36, :] = sig
    cells = [
        jnp.clip((jnp.clip(x[4 * a : 4 * a + 4], -1.0, 2.0) * 4.0).astype(jnp.int32), 0, 3)
        for a in range(3)
    ]
    index = row * TILE + lax.broadcasted_iota(jnp.int32, (4, TILE), 1)
    key = jnp.where(live, hilbert(cells, 2), 64) * 512 + index
    key = jnp.concatenate([key.astype(F32), jnp.zeros((4, TILE), F32)], 0)
    down = jnp.transpose(key, (1, 0))
    ranks = []
    for j in range(4):
        less = jnp.zeros((TILE, TILE), F32)
        for i in range(4):
            less = less + (down[:, i : i + 1] < key[j : j + 1, :]).astype(F32)
        ranks.append(jnp.sum(less, axis=0, keepdims=True))
    rank = jnp.concatenate(ranks, 0)
    fields = jnp.concatenate([stage[pl.ds(t, 16, stride=4), :] for t in range(4)], 1)
    parts = split3(fields)
    for t in range(4):
        out = lax.dot_general(
            parts, chosen(rank, t), (((1,), (1,)), ((), ())), preferred_element_type=F32
        )
        staged[pl.ds(t, 16, stride=4), :] = (out[32:48] + out[16:32]) + out[0:16]
    row16 = lax.broadcasted_iota(jnp.int32, (16, TILE), 0)
    place = staged[0:16, :]
    x_ref[...] = place
    v_ref[...] = staged[12:28, :]
    rec[0] = jnp.where((row16 & 3) < count, place, FAR)
    rec[0, 12:16, :] = rank
    rec[1] = jnp.where(row16 < 12, staged[24:40, :], count.astype(F32))
    meet(OFFSETS)
    copies = [
        send(rec, all_ref.at[k], send_sem.at[k], recv_sem.at[k], there(d, -1))
        for k, d in enumerate(OFFSETS)
    ]
    for copy in copies:
        copy.start()
    own = pltpu.make_async_copy(rec, all_ref.at[NBR], sem.at[8])
    own.start()
    own.wait()
    for copy in copies:
        copy.wait()


def turn_kernel(
    fout_ref, fown_ref, x_ref, v_ref, old_ref,
    nbr_ref, new_ref, x2_ref, v2_ref,
    back, send_sem, recv_sem, send2_sem, recv2_sem,
):
    hail(OFFSETS)
    meet(OFFSETS)
    copies = [
        send(fout_ref.at[k], back.at[k], send_sem.at[k], recv_sem.at[k], there(d, 1))
        for k, d in enumerate(OFFSETS)
    ]
    for copy in copies:
        copy.start()
    for copy in copies:
        copy.wait_recv()
    total = fown_ref[...]
    for k in range(NBR):
        total = total + back[k]
    v = v_ref[...] + HALF_STEP * total
    v = v + HALF_STEP * total
    x = x_ref[...] + TIME_STEP * v
    row16 = lax.broadcasted_iota(jnp.int32, (16, TILE), 0)
    new = jnp.where(old_ref[NBR, 0] > 0.1 * FAR, FAR, x)
    new = jnp.where(row16 == 12, back[NP + 1, 12:13, :], new)
    new = jnp.where(row16 == 13, back[NP, 12:13, :], new)
    new_ref[...] = jnp.where(row16 == 14, fown_ref[12:13, :], new)
    again = [
        send(new_ref, nbr_ref.at[k], send2_sem.at[k], recv2_sem.at[k], there(d, -1))
        for k, d in enumerate(OFFSETS)
    ]
    for copy in again:
        copy.start()
    x2_ref[...] = x
    v2_ref[...] = v
    for copy in copies:
        copy.wait_send()
    for copy in again:
        copy.wait()


def last_kernel(
    fout_ref, fown_ref, x_ref, v_ref, first_ref, xo_ref, vo_ref, fo_ref,
    back, stage, onehot, send_sem, recv_sem,
):
    hail(OFFSETS)
    meet(OFFSETS)
    copies = [
        send(fout_ref.at[k], back.at[k], send_sem.at[k], recv_sem.at[k], there(d, 1))
        for k, d in enumerate(OFFSETS)
    ]
    for copy in copies:
        copy.start()
    rank = first_ref[NBR, 0, 12:16, :]
    for t in range(4):
        onehot[TILE * t : TILE * t + TILE, :] = chosen(rank, t)
    for copy in copies:
        copy.wait()
    total = fown_ref[...]
    for k in range(NBR):
        total = total + back[k]
    stage[0:16, :] = x_ref[...]
    stage[12:28, :] = v_ref[...] + HALF_STEP * total
    stage[24:40, :] = total
    stage[36:64, :] = jnp.zeros((28, TILE), F32)
    fields = jnp.concatenate([stage[pl.ds(t, 16, stride=4), :] for t in range(4)], 1)
    out = jnp.dot(split3(fields), onehot[...], preferred_element_type=F32)
    out = (out[32:48] + out[16:32]) + out[0:16]
    for f in range(3):
        xo_ref[f, 0, 0] = out[f : f + 1]
        vo_ref[f, 0, 0] = out[3 + f : 4 + f]
        fo_ref[f, 0, 0] = out[6 + f : 7 + f]


def place_kernel(*refs):
    copies = [pltpu.make_async_copy(refs[i], refs[3 + i], refs[6].at[i]) for i in range(3)]
    for copy in copies:
        copy.start()
    for copy in copies:
        copy.wait()


def call(kernel, outs, scratch, collective=None, ins=None, raw_in=False, raw_out=False, limit=24 << 20):
    vmem = pl.BlockSpec(memory_space=pltpu.VMEM)
    hbm = pl.BlockSpec(memory_space=pltpu.HBM)
    params = {"vmem_limit_bytes": limit}
    if collective is not None:
        params.update(collective_id=collective, has_side_effects=True)
    return pl.pallas_call(
        kernel,
        out_shape=tuple(jax.ShapeDtypeStruct(shape, kind) for shape, kind in outs),
        in_specs=[hbm if raw_in else vmem] * ins,
        out_specs=tuple(hbm if raw_out else vmem for _ in outs),
        scratch_shapes=scratch,
        compiler_params=pltpu.CompilerParams(**params),
    )


def on_device(
    positions, velocities, forces, charges, atom_types, tile_counts, pair_epsilon, pair_sigma
):
    dma = pltpu.SemaphoreType.DMA((NBR,))
    rows = ((16, TILE), F32)
    wide = (positions, velocities, forces, charges, atom_types)
    small = (tile_counts, pair_epsilon, pair_sigma)
    x, v, first = call(
        first_kernel,
        (rows, rows, ((NBR + 1, 2, 16, TILE), F32)),
        [pltpu.VMEM(given.shape, given.dtype) for given in wide]
        + [pltpu.SMEM(given.shape, given.dtype) for given in small]
        + [pltpu.VMEM((64, TILE), F32), pltpu.VMEM((64, TILE), F32), pltpu.VMEM((2, 16, TILE), F32),
           pltpu.SemaphoreType.DMA((9,)), dma, dma],
        collective=0,
        ins=8,
        raw_in=True,
        limit=67043328,
    )(
        *wide, *small
    )
    fout, fown = pair_forces(first, first, first, True)
    second, own, x, v = call(
        turn_kernel,
        (((NBR, 16, TILE), F32), rows, rows, rows),
        [pltpu.VMEM((NBR, 16, TILE), F32), dma, dma, dma, dma],
        collective=1,
        ins=5,
    )(fout, fown, x, v, first)
    fout, fown = pair_forces(second, first, own, False)
    flat = ((3, 1, 1, 1, 4 * TILE), F32)
    outs = call(
        last_kernel,
        (flat, flat, flat),
        [pltpu.VMEM((NBR, 16, TILE), F32), pltpu.VMEM((64, TILE), F32),
         pltpu.VMEM((512, 512), BF16), dma, dma],
        collective=2,
        ins=5,
    )(fout, fown, x, v, first)
    return call(
        place_kernel, (flat, flat, flat), [pltpu.SemaphoreType.DMA((3,))], ins=3, raw_out=True
    )(*outs)


def solution(mesh):
    atoms = P(None, "gx", "gy", "gz", None)
    in_specs = (
        atoms, atoms, atoms,
        P("gx", "gy", "gz", None),
        P("gx", "gy", "gz", None),
        P("gx", "gy", "gz"),
        P(), P(),
    )
    return jax.shard_map(
        on_device, mesh=mesh, in_specs=in_specs, out_specs=(atoms,) * 3, check_vma=False
    )
```

```python
import functools

import jax
import jax.numpy as jnp
from jax import lax
from jax.experimental import pallas as pl
from jax.experimental.pallas import tpu as pltpu
from jax.sharding import PartitionSpec as P

TILE = 128
STEPS = 2
TIME_STEP = 0.05
HALF_STEP = 0.025
PLATE = ((1, 0), (1, 1), (0, 1), (-1, 1), (-1, 0), (-1, -1), (0, -1), (1, -1))
NP = len(PLATE)
OFFSETS = tuple((x, y, 0) for x, y in PLATE) + ((0, 0, -1), (0, 0, 1))
NBR = NP + 2
AXES = ("gx", "gy", "gz")
MESH = pl.DeviceIdType.MESH
F32 = jnp.float32
BF16 = jnp.bfloat16
FAR = 1e6
RIGHTS = 4 * (NP + 2)
RROWS = RIGHTS + 8
UNROLL = 10
PAD = 12
LOG2E = 1.4426950408889634
FORCE = 8.0 / (3.24 * 3.24)


def shares(first, pos_ref, par_ref, own_ref):
    row = lax.broadcasted_iota(jnp.int32, (64, TILE), 0)
    col = lax.broadcasted_iota(jnp.int32, (64, TILE), 1)
    lane = lax.broadcasted_iota(jnp.int32, (1, TILE), 1) >> 2
    lt, lbox, rt, rbox = row >> 4, (row >> 2) & 3, col & 3, col >> 2
    own_n = par_ref[NBR, 1, 12:13, :]
    nr = own_n
    for j in range(NP):
        nr = jnp.where(lane == j, par_ref[j, 1, 12:13, :], nr)
    below_n, above_n = par_ref[NP, 1, 12:13, :], par_ref[NP + 1, 1, 12:13, :]
    nl = jnp.where(lbox == 0, below_n, jnp.where(lbox == 2, above_n, own_n))
    nr = jnp.broadcast_to(nr, (64, TILE))
    ahead = (rbox < NP // 2) | ((rbox == NP) & (lbox == 2))
    left_first = (rbox < NP // 2) | ((rbox == NP) & (lbox == 0))
    lf, rf = lt.astype(F32), rt.astype(F32)
    order = jnp.where(left_first, lf * nr + rf, rf * nl + lf)
    if first:
        w1 = jnp.where(left_first, nl, nr)
        w2 = jnp.where(left_first, nr, nl)
    else:
        mine = own_ref[14:15, :]
        below, same, above = mine, mine, mine
        for j in range(NP):
            hit = lane == j
            below = jnp.where(hit, pos_ref[j, 12:13, :], below)
            same = jnp.where(hit, pos_ref[j, 14:15, :], same)
            above = jnp.where(hit, pos_ref[j, 13:14, :], above)
        below = jnp.where(lane == NP, pos_ref[NP, 14:15, :], below)
        above = jnp.where(lane == NP, pos_ref[NP + 1, 14:15, :], above)
        other = jnp.where(lbox == 0, below, jnp.where(lbox == 2, above, same))
        mine = jnp.broadcast_to(mine, (64, TILE))
        w1 = jnp.where(ahead, mine, other)
        w2 = jnp.where(ahead, other, mine)
    w1, w2 = w1 * w1 * w1, w2 * w2 * w2
    inside = (order + 0.5) * (w1 + w2) < w2 * (nl * nr)
    takes = jnp.where(inside, 1.0, 0.0)
    takes = jnp.where(ahead, takes, 1.0 - takes)
    shared = ((rbox < NP) & (lbox < 3)) | ((rbox == NP) & ((lbox == 0) | (lbox == 2)))
    alone = ((rbox == NP) & (lbox == 1) & (lt < rt)) | ((rbox == NP + 1) & (lbox == 1) & (lt == rt))
    return jnp.where(shared, takes, jnp.where(alone, 1.0, -1.0))


def pair_kernel(
    joined, pos_ref, par_ref, own_ref, fout_ref, fown_ref,
    left, right, acc_left, acc_right, list_v, list_s, sem,
):
    position = (lambda k: pos_ref[k, 0]) if joined else (lambda k: pos_ref[k])
    own = own_ref[NBR, 0] if joined else own_ref[...]
    row16 = lax.broadcasted_iota(jnp.int32, (16, 1), 0)
    lane16 = lax.broadcasted_iota(jnp.int32, (1, 16), 1)
    for k in range(NP + 2):
        if k < NP:
            p = position(k) + jnp.where(
                row16 < 4, float(PLATE[k][0]), jnp.where(row16 < 8, float(PLATE[k][1]), 0.0)
            )
            a = par_ref[k, 1]
        else:
            p, a = own, par_ref[NBR, 1]
        p = p * 2.0
        for f in range(3):
            right[f, 4 * k : 4 * k + 4, :] = p[4 * f : 4 * f + 4]
            right[3 + f, 4 * k : 4 * k + 4, :] = a[4 * f : 4 * f + 4]
    for f in range(6):
        right[f, RIGHTS:RROWS, :] = jnp.full((8, TILE), FAR if f < 3 else 0.0, F32)
    mins, maxs, downs = [], [], []
    scale = jnp.where(lane16 < 4, 0.04 / 6.0 * FORCE, jnp.where(lane16 < 8, 4.0 * FORCE, 1.0))
    for box in range(3):
        if box == 1:
            p, a = own, par_ref[NBR, 1]
        else:
            slot = NP if box == 0 else NP + 1
            p = position(slot) + jnp.where(
                (row16 >= 8) & (row16 < 12), -1.0 if box == 0 else 1.0, 0.0
            )
            a = par_ref[slot, 1]
        down = jnp.transpose(jnp.concatenate([p * 2.0, a], 0), (1, 0))
        blocks = down[:, :16].reshape(4, 32, 16)
        mins.append(jnp.min(blocks, axis=1))
        maxs.append(jnp.max(blocks, axis=1))
        downs.append(down)
    far = jnp.full((4, 16), FAR, F32)
    low = jnp.concatenate(mins + [far], 0)
    high = jnp.concatenate(maxs + [far], 0)
    gaps = jnp.zeros((64, TILE), F32)
    alive = None
    for f in range(3):
        a0 = jnp.concatenate([low[:, 4 * f + t : 4 * f + t + 1] for t in range(4)], 0)
        a1 = jnp.concatenate([high[:, 4 * f + t : 4 * f + t + 1] for t in range(4)], 0)
        v = jnp.concatenate([right[f], jnp.full((TILE - RROWS, TILE), FAR, F32)], 0)
        b0 = jnp.broadcast_to(jnp.min(v, axis=1, keepdims=True), (TILE, TILE))
        b1 = jnp.broadcast_to(jnp.max(v, axis=1, keepdims=True), (TILE, TILE))
        b0 = jnp.transpose(b0, (1, 0))[:1]
        b1 = jnp.transpose(b1, (1, 0))[:1]
        gap = jnp.maximum(jnp.maximum(a0 - b1, b0 - a1), 0.0)
        gaps = gaps + gap * gap
        if f == 0:
            alive = a0 < 0.1 * FAR
    mine = shares(joined, pos_ref, par_ref, own_ref)
    close = (gaps < 3.2401) & alive
    near = close & (mine > 0.5)
    weight = jnp.sum(jnp.where(close & (mine > -0.5), 1.0, 0.0), axis=0, keepdims=True)
    weight = jnp.sum(weight, axis=1, keepdims=True) + 1.0
    row = lax.broadcasted_iota(jnp.int32, (64, TILE), 0)
    r64 = lax.broadcasted_iota(jnp.int32, (64, 64), 0)
    c64 = lax.broadcasted_iota(jnp.int32, (64, 64), 1)
    ones = near.astype(F32)
    before = jnp.dot(
        (c64 < r64).astype(F32).astype(BF16), ones.astype(BF16), preferred_element_type=F32
    )
    place = jnp.where(near, before.astype(jnp.int32), -1)
    lane = lax.broadcasted_iota(jnp.int32, (8, TILE), 1)
    count = jnp.broadcast_to(jnp.sum(ones, axis=0, keepdims=True), (8, TILE))
    total = jnp.sum(count[:1], axis=1, keepdims=True)
    named = jnp.where((count > 0.5) & (lane < RIGHTS), lane.astype(F32), float(RIGHTS))
    after = pltpu.roll(named, TILE - 1, 1)
    for step in (1, 2, 4, 8, 16, 32):
        after = jnp.minimum(after, pltpu.roll(after, TILE - step, 1))
    count = jnp.where(lane < RIGHTS, count, 1e6).astype(jnp.int32)[:1]
    value = row - PAD
    for w in range(12):
        word = jnp.zeros((1, TILE), jnp.int32)
        for j in range(4):
            hit = jnp.where(place == 4 * w + j, value, 0)
            word = word + (jnp.sum(hit, axis=0, keepdims=True) + PAD) * (64**j)
        list_v[w : w + 1, :] = word
    list_v[12:13, :] = count
    list_v[13:14, :] = jnp.broadcast_to(total, (1, TILE)).astype(jnp.int32)
    list_v[14:15, :] = after[:1].astype(jnp.int32)
    list_v[15:16, :] = jnp.minimum(named, after)[:1].astype(jnp.int32)
    copy = pltpu.make_async_copy(list_v, list_s, sem)
    copy.start()
    wanted = (lax.broadcasted_iota(jnp.int32, (48, 4 * TILE), 0) & 15) - (
        lax.broadcasted_iota(jnp.int32, (48, 4 * TILE), 1) >> 7
    )
    picks = [jnp.where(wanted == 4 * f, 1.0, 0.0).astype(BF16) for f in range(3)]
    for box, down in enumerate(downs):
        scaled = down[:, 16:] * scale
        for f in range(0, 6):
            source = down[:, :16] if f < 3 else scaled
            hi = source.astype(BF16)
            rest = source - hi.astype(F32)
            mid = rest.astype(BF16)
            pieces = jnp.concatenate([hi, mid, (rest - mid.astype(F32)).astype(BF16)], 1)
            wide = jnp.dot(pieces, picks[f % 3], preferred_element_type=F32)
            for t in range(4):
                base = (t * 16 + box * 4) * 4
                left[f, base : base + 16] = wide[:, TILE * t : TILE * t + TILE].reshape(16, 8, TILE)
    for f in range(6):
        left[f, 4 * PAD : 4 * PAD + 4] = jnp.full((4, 8, TILE), FAR if f < 3 else 0.0, F32)
    acc_left[...] = jnp.zeros_like(acc_left)
    acc_right[...] = jnp.zeros_like(acc_right)
    copy.wait()

    def turn(_, state):
        r, k = state
        for _ in range(UNROLL):
            b = ((list_s[k >> 2, r] >> ((k & 3) * 6)) & 63) * 4
            at = pl.ds(b, 4)
            rx, ry, rz, rq, re, rs_ = [
                jnp.broadcast_to(right[f, pl.ds(r, 1), :], (8, TILE))[None] for f in range(6)
            ]
            dx = left[0, at] - rx
            dy = left[1, at] - ry
            dz = left[2, at] - rz
            s2 = (dx * dx + 0.09) + dy * dy + dz * dz
            rs = lax.rsqrt(s2)
            inv = rs * rs
            screen = jnp.exp2(s2 * (-LOG2E) * rs)
            w = jnp.maximum(3.33 - s2, 0.0)
            slope = (w * inv) * 1.5
            one = slope + 1.0
            two = one + slope
            size = left[5, at] + rs_
            ratio = size * size * inv
            cubed = ratio * ratio * ratio
            lennard = (left[4, at] * re) * cubed * (cubed * two - one)
            coulomb = (left[3, at] * rq) * screen * (rs * (one + 5.0) + slope)
            g = (lennard + coulomb) * w
            fx, fy, fz = g * dx, g * dy, g * dz
            acc_left[0, at] += fx
            acc_left[1, at] += fy
            acc_left[2, at] += fz
            acc_right[0, r] -= jnp.sum(fx, axis=0)
            acc_right[1, r] -= jnp.sum(fy, axis=0)
            acc_right[2, r] -= jnp.sum(fz, axis=0)
            on = k + 1 >= list_s[12, r]
            k = jnp.where(on, 0, k + 1)
            r = jnp.where(on, list_s[14, r], r)
        return r, k

    lax.fori_loop(0, (list_s[13, 0] + UNROLL - 1) // UNROLL, turn, (list_s[15, 0], jnp.int32(0)))
    tail = jnp.broadcast_to(weight, (4, TILE))

    def gathered(k):
        rows = [jnp.sum(acc_right[f, 4 * k : 4 * k + 4], axis=1) for f in range(3)]
        return jnp.concatenate(rows + [tail], 0)

    for k in range(NP):
        fout_ref[k] = gathered(k)
    ones = [
        jnp.where(lax.broadcasted_iota(jnp.int32, (2 * TILE, TILE), 1) == f, 1.0, 0.0).astype(BF16)
        for f in range(3)
    ]
    ones = jnp.concatenate(ones, 0)
    for box in range(3):
        parts = []
        for t in range(4):
            base = (t * 16 + box * 4) * 4
            halves = []
            for f in range(3):
                a = acc_left[f, base : base + 16].reshape(TILE, TILE)
                hi = a.astype(BF16)
                halves += [hi, (a - hi.astype(F32)).astype(BF16)]
            parts.append(jnp.concatenate(halves, 1))
        sums = jnp.dot(jnp.concatenate(parts, 0), ones, preferred_element_type=F32)
        target = fown_ref if box == 1 else fout_ref.at[NP if box == 0 else NP + 1]
        other = gathered(NP)
        for t in range(4):
            row = jnp.transpose(sums[TILE * t : TILE * t + TILE], (1, 0))
            for f in range(3):
                at = 4 * f + t
                value = row[f : f + 1]
                target[at : at + 1, :] = value + other[at : at + 1] if box == 1 else value
        target[12:16, :] = tail


def pair_forces(pos, par, own, joined):
    vmem = pl.BlockSpec(memory_space=pltpu.VMEM)
    return pl.pallas_call(
        functools.partial(pair_kernel, joined),
        out_shape=(
            jax.ShapeDtypeStruct((NBR, 16, TILE), F32),
            jax.ShapeDtypeStruct((16, TILE), F32),
        ),
        in_specs=[vmem] * 3,
        out_specs=(vmem, vmem),
        scratch_shapes=[
            pltpu.VMEM((6, 256, 8, TILE), F32),
            pltpu.VMEM((6, RROWS, TILE), F32),
            pltpu.VMEM((3, 256, 8, TILE), F32),
            pltpu.VMEM((3, RROWS, 8, TILE), F32),
            pltpu.VMEM((16, TILE), jnp.int32),
            pltpu.SMEM((16, TILE), jnp.int32),
            pltpu.SemaphoreType.DMA,
        ],
        compiler_params=pltpu.CompilerParams(vmem_limit_bytes=24 << 20),
    )(pos, par, own)


def hilbert(cells, bits):
    x = list(cells)
    q = 1 << (bits - 1)
    while q > 1:
        p = q - 1
        for i in range(3):
            hit = (x[i] & q) != 0
            if i == 0:
                x[0] = jnp.where(hit, x[0] ^ p, x[0])
            else:
                swap = (x[0] ^ x[i]) & p
                x[0], x[i] = jnp.where(hit, x[0] ^ p, x[0] ^ swap), jnp.where(hit, x[i], x[i] ^ swap)
        q >>= 1
    x[1] = x[1] ^ x[0]
    x[2] = x[2] ^ x[1]
    flip = jnp.zeros_like(x[0])
    q = 1 << (bits - 1)
    while q > 1:
        flip = jnp.where((x[2] & q) != 0, flip ^ (q - 1), flip)
        q >>= 1
    x = [v ^ flip for v in x]
    key = jnp.zeros_like(x[0])
    for bit in range(bits - 1, -1, -1):
        for a in range(3):
            key = key * 2 + ((x[a] >> bit) & 1)
    return key


def split3(a):
    hi = a.astype(BF16)
    rest = a - hi.astype(F32)
    mid = rest.astype(BF16)
    lo = (rest - mid.astype(F32)).astype(BF16)
    return jnp.concatenate([hi, mid, lo], 0)


def chosen(rank, t):
    place = (lax.broadcasted_iota(jnp.int32, (TILE, TILE), 0) + TILE * t).astype(F32)
    tiles = [(rank[j : j + 1, :] == place).astype(F32).astype(BF16) for j in range(4)]
    return jnp.concatenate(tiles, 1)


def there(offset, sign):
    return tuple(
        lax.rem(lax.axis_index(a) + sign * o + lax.axis_size(a), lax.axis_size(a))
        for a, o in zip(AXES, offset)
    )


def hail(offsets):
    barrier = pltpu.get_barrier_semaphore()
    for d in offsets:
        pl.semaphore_signal(barrier, inc=1, device_id=there(d, 1), device_id_type=MESH)


def meet(offsets):
    pl.semaphore_wait(pltpu.get_barrier_semaphore(), len(offsets))


def send(source, target, send_sem, recv_sem, device):
    return pltpu.make_async_remote_copy(
        src_ref=source,
        dst_ref=target,
        send_sem=send_sem,
        recv_sem=recv_sem,
        device_id=device,
        device_id_type=MESH,
    )


def first_kernel(*refs):
    given, (x_ref, v_ref, all_ref), held = refs[:8], refs[8:11], refs[11:19]
    stage, staged, rec, sem, send_sem, recv_sem = refs[19:]
    hail(OFFSETS)
    copies = [
        pltpu.make_async_copy(source, target, sem.at[i])
        for i, (source, target) in enumerate(zip(given, held))
    ]
    for copy in copies:
        copy.start()
    for copy in copies:
        copy.wait()
    pos_ref, vel_ref, frc_ref, chg_ref, typ_ref, count_ref, eps_ref, sig_ref = held

    def rows(ref, f):
        return [ref[f, 0, 0, :, TILE * t : TILE * t + TILE] for t in range(4)]

    def rows1(ref):
        return [ref[0, 0, :, TILE * t : TILE * t + TILE] for t in range(4)]

    def flat(ref):
        return jnp.concatenate([row for f in range(3) for row in rows(ref, f)], 0)

    v = flat(vel_ref) + HALF_STEP * flat(frc_ref)
    x = flat(pos_ref) + TIME_STEP * v
    count = count_ref[0, 0, 0]
    row = lax.broadcasted_iota(jnp.int32, (4, TILE), 0)
    live = row < count
    kinds = jnp.concatenate(rows1(typ_ref), 0)
    eps = jnp.zeros((4, TILE), F32)
    sig = jnp.zeros((4, TILE), F32)
    for k in range(eps_ref.shape[0]):
        eps = jnp.where(kinds == k, eps_ref[k], eps)
        sig = jnp.where(kinds == k, sig_ref[k], sig)
    alive = live.astype(F32)
    stage[...] = jnp.zeros_like(stage)
    stage[0:12, :] = x
    stage[12:24, :] = v
    stage[24:28, :] = jnp.concatenate(rows1(chg_ref), 0) * alive
    stage[28:32, :] = jnp.sqrt(eps) * alive
    stage[32:36, :] = sig
    cells = [
        jnp.clip((jnp.clip(x[4 * a : 4 * a + 4], -1.0, 2.0) * 4.0).astype(jnp.int32), 0, 3)
        for a in range(3)
    ]
    index = row * TILE + lax.broadcasted_iota(jnp.int32, (4, TILE), 1)
    key = jnp.where(live, hilbert(cells, 2), 64) * 512 + index
    key = jnp.concatenate([key.astype(F32), jnp.zeros((4, TILE), F32)], 0)
    down = jnp.transpose(key, (1, 0))
    ranks = []
    for j in range(4):
        less = jnp.zeros((TILE, TILE), F32)
        for i in range(4):
            less = less + (down[:, i : i + 1] < key[j : j + 1, :]).astype(F32)
        ranks.append(jnp.sum(less, axis=0, keepdims=True))
    rank = jnp.concatenate(ranks, 0)
    fields = jnp.concatenate([stage[pl.ds(t, 16, stride=4), :] for t in range(4)], 1)
    parts = split3(fields)
    for t in range(4):
        out = lax.dot_general(
            parts, chosen(rank, t), (((1,), (1,)), ((), ())), preferred_element_type=F32
        )
        staged[pl.ds(t, 16, stride=4), :] = (out[32:48] + out[16:32]) + out[0:16]
    row16 = lax.broadcasted_iota(jnp.int32, (16, TILE), 0)
    place = staged[0:16, :]
    x_ref[...] = place
    v_ref[...] = staged[12:28, :]
    rec[0] = jnp.where((row16 & 3) < count, place, FAR)
    rec[0, 12:16, :] = rank
    rec[1] = jnp.where(row16 < 12, staged[24:40, :], count.astype(F32))
    meet(OFFSETS)
    copies = [
        send(rec, all_ref.at[k], send_sem.at[k], recv_sem.at[k], there(d, -1))
        for k, d in enumerate(OFFSETS)
    ]
    for copy in copies:
        copy.start()
    own = pltpu.make_async_copy(rec, all_ref.at[NBR], sem.at[8])
    own.start()
    own.wait()
    for copy in copies:
        copy.wait()


def turn_kernel(
    fout_ref, fown_ref, x_ref, v_ref, old_ref,
    nbr_ref, new_ref, x2_ref, v2_ref,
    back, send_sem, recv_sem, send2_sem, recv2_sem,
):
    hail(OFFSETS)
    meet(OFFSETS)
    copies = [
        send(fout_ref.at[k], back.at[k], send_sem.at[k], recv_sem.at[k], there(d, 1))
        for k, d in enumerate(OFFSETS)
    ]
    for copy in copies:
        copy.start()
    for copy in copies:
        copy.wait_recv()
    total = fown_ref[...]
    for k in range(NBR):
        total = total + back[k]
    v = v_ref[...] + HALF_STEP * total
    v = v + HALF_STEP * total
    x = x_ref[...] + TIME_STEP * v
    row16 = lax.broadcasted_iota(jnp.int32, (16, TILE), 0)
    new = jnp.where(old_ref[NBR, 0] > 0.1 * FAR, FAR, x)
    new = jnp.where(row16 == 12, back[NP + 1, 12:13, :], new)
    new = jnp.where(row16 == 13, back[NP, 12:13, :], new)
    new_ref[...] = jnp.where(row16 == 14, fown_ref[12:13, :], new)
    again = [
        send(new_ref, nbr_ref.at[k], send2_sem.at[k], recv2_sem.at[k], there(d, -1))
        for k, d in enumerate(OFFSETS)
    ]
    for copy in again:
        copy.start()
    x2_ref[...] = x
    v2_ref[...] = v
    for copy in copies:
        copy.wait_send()
    for copy in again:
        copy.wait()


def last_kernel(
    fout_ref, fown_ref, x_ref, v_ref, first_ref, xo_ref, vo_ref, fo_ref,
    back, stage, onehot, send_sem, recv_sem,
):
    hail(OFFSETS)
    meet(OFFSETS)
    copies = [
        send(fout_ref.at[k], back.at[k], send_sem.at[k], recv_sem.at[k], there(d, 1))
        for k, d in enumerate(OFFSETS)
    ]
    for copy in copies:
        copy.start()
    rank = first_ref[NBR, 0, 12:16, :]
    for t in range(4):
        onehot[TILE * t : TILE * t + TILE, :] = chosen(rank, t)
    for copy in copies:
        copy.wait()
    total = fown_ref[...]
    for k in range(NBR):
        total = total + back[k]
    stage[0:16, :] = x_ref[...]
    stage[12:28, :] = v_ref[...] + HALF_STEP * total
    stage[24:40, :] = total
    stage[36:64, :] = jnp.zeros((28, TILE), F32)
    fields = jnp.concatenate([stage[pl.ds(t, 16, stride=4), :] for t in range(4)], 1)
    out = jnp.dot(split3(fields), onehot[...], preferred_element_type=F32)
    out = (out[32:48] + out[16:32]) + out[0:16]
    for f in range(3):
        xo_ref[f, 0, 0] = out[f : f + 1]
        vo_ref[f, 0, 0] = out[3 + f : 4 + f]
        fo_ref[f, 0, 0] = out[6 + f : 7 + f]


def place_kernel(*refs):
    copies = [pltpu.make_async_copy(refs[i], refs[3 + i], refs[6].at[i]) for i in range(3)]
    for copy in copies:
        copy.start()
    for copy in copies:
        copy.wait()


def call(kernel, outs, scratch, collective=None, ins=None, raw_in=False, raw_out=False, limit=24 << 20):
    vmem = pl.BlockSpec(memory_space=pltpu.VMEM)
    hbm = pl.BlockSpec(memory_space=pltpu.HBM)
    params = {"vmem_limit_bytes": limit}
    if collective is not None:
        params.update(collective_id=collective, has_side_effects=True)
    return pl.pallas_call(
        kernel,
        out_shape=tuple(jax.ShapeDtypeStruct(shape, kind) for shape, kind in outs),
        in_specs=[hbm if raw_in else vmem] * ins,
        out_specs=tuple(hbm if raw_out else vmem for _ in outs),
        scratch_shapes=scratch,
        compiler_params=pltpu.CompilerParams(**params),
    )


def on_device(
    positions, velocities, forces, charges, atom_types, tile_counts, pair_epsilon, pair_sigma
):
    dma = pltpu.SemaphoreType.DMA((NBR,))
    rows = ((16, TILE), F32)
    wide = (positions, velocities, forces, charges, atom_types)
    small = (tile_counts, pair_epsilon, pair_sigma)
    x, v, first = call(
        first_kernel,
        (rows, rows, ((NBR + 1, 2, 16, TILE), F32)),
        [pltpu.VMEM(given.shape, given.dtype) for given in wide]
        + [pltpu.SMEM(given.shape, given.dtype) for given in small]
        + [pltpu.VMEM((64, TILE), F32), pltpu.VMEM((64, TILE), F32), pltpu.VMEM((2, 16, TILE), F32),
           pltpu.SemaphoreType.DMA((9,)), dma, dma],
        collective=0,
        ins=8,
        raw_in=True,
        limit=67043328,
    )(
        *wide, *small
    )
    fout, fown = pair_forces(first, first, first, True)
    second, own, x, v = call(
        turn_kernel,
        (((NBR, 16, TILE), F32), rows, rows, rows),
        [pltpu.VMEM((NBR, 16, TILE), F32), dma, dma, dma, dma],
        collective=1,
        ins=5,
    )(fout, fown, x, v, first)
    fout, fown = pair_forces(second, first, own, False)
    flat = ((3, 1, 1, 1, 4 * TILE), F32)
    outs = call(
        last_kernel,
        (flat, flat, flat),
        [pltpu.VMEM((NBR, 16, TILE), F32), pltpu.VMEM((64, TILE), F32),
         pltpu.VMEM((512, 512), BF16), dma, dma],
        collective=2,
        ins=5,
    )(fout, fown, x, v, first)
    return call(
        place_kernel, (flat, flat, flat), [pltpu.SemaphoreType.DMA((3,))], ins=3, raw_out=True
    )(*outs)


def solution(mesh):
    atoms = P(None, "gx", "gy", "gz", None)
    in_specs = (
        atoms, atoms, atoms,
        P("gx", "gy", "gz", None),
        P("gx", "gy", "gz", None),
        P("gx", "gy", "gz"),
        P(), P(),
    )
    return jax.shard_map(
        on_device, mesh=mesh, in_specs=in_specs, out_specs=(atoms,) * 3, check_vma=False
    )
```
